512 devices in a mesh: dp: 8 (over x, core), seq: 64 (over z, y).
Axes of the slice: x: 4, y: 4, z: 16, core: 2. Of those that a mesh axis runs over, the one named last changes fastest.
Arguments:
- queries: bfloat16 [65536, 2048], P(('dp', 'seq')), may hold values from -170 to 170
- database: bfloat16 [2048, 8, 896], P('seq'), may hold values from -90 to 90
- enc_gain: float32 [896], replicated, may hold values from 0.1 to 1.9
- key_weight: bfloat16 [896, 2048], P(None, 'dp'), may hold values from -0.1875 to 0.1875
- value_weight: bfloat16 [896, 2048], P(None, 'dp'), may hold values from -0.1875 to 0.1875
- ret_shard: int32 [1024, 16], P(('dp', 'seq')), may hold values from 0 to 63, all different within a row; in each aligned block of 2 rows (0 to 1, 2 to 3, ...) at most 2 rows name the same one
- ret_row: int32 [1024, 16], P(('dp', 'seq')), may hold values from 0 to 31
Outputs:
- attended: bfloat16 [65536, 2048], P(('dp', 'seq'))
The draws below stay inside these ranges and needn't reach their ends.
Inputs may be any that keep to these rules, and one draw needn't show every extreme that they name: `ret_shard`: the 16 neighbours of one span name different shards; among the 32 entries of the spans of one device, at most 2 name one shard, and exactly 2 do so for some shard in some devices.
All inputs are finite; a program needn't handle non-finite values.
Results may differ from the reference program's by a relative error of at most 0.008.
Values may be sent and summed in bfloat16 or wider, within the bound.
A program may use at most 64 MiB of HBM per device.

```python
import math
import jax
import jax.numpy as jnp
import numpy as np
from jax import lax

D_ENC = 896
HEADS = 16
DH = 128
SPAN = 64
NBRS = 16
NBR_LEN = 8
CH_DEV = 2
DB_DEV = 32
CAP = 2
SPANS = 1024
TOKENS = 65536
DB_ROWS = 2048
N_SEQ = 64


def draw_queries(key, part):
    shape = (TOKENS, HEADS * DH)
    first = jax.random.fold_in(key, 0)
    base = jnp.clip(jax.random.normal(first, shape, jnp.float32), -6.0, 6.0)
    return base.astype(jnp.bfloat16)


def draw_database(key, part):
    shape = (DB_ROWS, NBR_LEN, D_ENC)
    first, second, third = jax.random.split(key, 3)
    row_scale = jnp.exp(jax.random.uniform(second, (DB_ROWS, NBR_LEN, 1), jnp.float32, math.log(0.3), math.log(3.0)))
    col_scale = jnp.exp(jax.random.uniform(third, (1, 1, D_ENC), jnp.float32, math.log(0.5), math.log(5.0)))
    base = jnp.clip(jax.random.normal(first, shape, jnp.float32), -6.0, 6.0)
    return (base * row_scale * col_scale).astype(jnp.bfloat16)


def with_ends(values, key, low, top_value):
    longest = values.shape.index(max(values.shape))
    spots = []
    for shift in (0, 1):
        where = [jax.random.randint(jax.random.fold_in(key, axis), (), 0, length) for axis, length in enumerate(values.shape)]
        where[longest] = (where[longest] + shift) % values.shape[longest]
        spots.append(tuple(where))
    return values.at[spots[0]].set(low).at[spots[1]].set(top_value)


def block_scale(rng, shape, cuts, low, top_value):
    def one(axis_at, shards_of):
        heights = jax.random.uniform(jax.random.fold_in(jax.random.fold_in(rng, 6), axis_at), (shards_of,), jnp.float32, low / len(cuts), top_value / len(cuts))
        return jnp.repeat(jnp.exp(heights), shape[axis_at] // shards_of).reshape((-1,) + (1,) * (len(shape) - axis_at - 1))

    level = one(*cuts[0])
    for cut in cuts[1:]:
        level = level * one(*cut)
    return level


def shared_out(rng, own, number, rows, count, top, reach, slope):
    order = jax.random.permutation(rng, count)
    heavy_load, ordinary = portions_of(count, rows * top, reach, slope, True), portions_of(count, rows * top, reach, slope, False)
    places = jnp.arange(count)

    def named(tallies, offset_by):
        used = int((tallies > 0).sum())
        fixed = max(1, used // 4)
        shifted = fixed + (places - fixed + offset_by * (used - fixed)) % max(1, count - fixed)
        return jnp.zeros((count,), jnp.int32).at[order[jnp.where(places < fixed, places, shifted)]].set(jnp.asarray(tallies, jnp.int32))

    tallies = jnp.where(number % 4 == 0, named(heavy_load, number // 4), named(ordinary, number - number // 4 - 1))
    mixed = jax.random.permutation(jax.random.fold_in(own, 3), count)
    source_of, taker = mixed[0:count // 2 * 2:2], mixed[1:count // 2 * 2:2]
    room = jnp.minimum(tallies[source_of] - 1, reach - tallies[taker]) // 2
    room = jnp.where((source_of == order[0]) | (taker == order[0]) | (tallies[taker] == 0), 0, jnp.maximum(room, 0))
    shifted = jax.random.randint(jax.random.fold_in(own, 4), (count // 2,), 0, 1 << 20) % (room + 1)
    tallies = tallies.at[source_of].add(-shifted).at[taker].add(shifted)
    members = jnp.searchsorted(jnp.cumsum(tallies), jnp.arange(rows * top), side="right").astype(jnp.int32)
    listing = members.reshape(top, rows).T
    listing = listing[jax.random.permutation(jax.random.fold_in(own, 1), rows)]
    offset_by = jax.random.randint(jax.random.fold_in(own, 2), (rows, 1), 0, top)
    return jnp.take_along_axis(listing, (jnp.arange(top)[None, :] + offset_by) % top, axis=1)


def portions_of(number_of, total, limit, skew, full):
    weights = [(1 << 20) // math.isqrt(standing ** skew) + 1 for standing in range(1, number_of + 1)]
    largest = limit if full else min(limit, max(-(-total // number_of), total * weights[0] // sum(weights)))
    least = 1 if total - largest >= number_of - 1 else 0
    given, surplus = [largest] + [least] * (number_of - 1), total - largest - least * (number_of - 1)
    while surplus > 0:
        movable = [i for i in range(1, number_of) if given[i] < largest] or [i for i in range(1, number_of) if given[i] < limit]
        pool, budget = sum([weights[i] for i in movable]), surplus
        for i in movable:
            addition = min(limit - given[i], max(1, budget * weights[i] // pool), surplus)
            given[i] = given[i] + addition
            surplus = surplus - addition
    return np.array(given)


def scatter_about(stream_key, dims, deviation, most, cuts=(), kind=jnp.bfloat16):
    values = deviation * jax.random.normal(stream_key, dims, jnp.float32)
    if cuts:
        values = values * block_scale(stream_key, dims, cuts, -0.22, 0.18)
    return jnp.clip(values, -most, most).astype(kind)


def setup_inputs(seed: int = 0) -> dict:
    seeds = jax.random.split(jax.random.key(seed), 8)
    queries = draw_queries(jax.random.fold_in(seeds[7], 71), 0)
    database = draw_database(jax.random.fold_in(seeds[7], 71), 0)
    enc_gain = jnp.clip(1.0 + 0.18 * jax.random.normal(seeds[2], (D_ENC,), jnp.float32), 0.1, 1.9)
    key_weight = scatter_about(seeds[3], (D_ENC, HEADS * DH), D_ENC ** -0.5, 0.1875, ((1, 8),))
    value_weight = scatter_about(seeds[4], (D_ENC, HEADS * DH), D_ENC ** -0.5, 0.1875, ((1, 8),))
    ret_shard_keys = jax.random.split(jax.random.fold_in(seeds[5], 1), SPANS // CH_DEV)
    ret_shard_turns = jax.random.permutation(jax.random.fold_in(seeds[5], 3), SPANS // CH_DEV)
    ret_shard = jax.vmap(lambda own, number: shared_out(jax.random.fold_in(seeds[5], 2), own, number, CH_DEV, N_SEQ, NBRS, CAP, 2))(ret_shard_keys, ret_shard_turns).reshape((SPANS, NBRS))
    ret_row = with_ends(jax.random.randint(seeds[6], (SPANS, NBRS), 0, DB_DEV), jax.random.fold_in(seeds[6], 1), 0, DB_DEV - 1).astype(jnp.int32)
    return {"queries": queries, "database": database, "enc_gain": enc_gain, "key_weight": key_weight, "value_weight": value_weight, "ret_shard": ret_shard, "ret_row": ret_row}


eps_norm = 1e-06

def encode(nbr_rows, enc_gain, key_weight, value_weight):
    group_count = nbr_rows.shape[0]
    widened = nbr_rows.astype(jnp.float32)
    mean_square = lax.optimization_barrier(jnp.mean(widened * widened, axis=-1, keepdims=True))
    normed = (widened * lax.rsqrt(mean_square + eps_norm) * enc_gain.astype(jnp.float32)).astype(jnp.bfloat16)
    flat_rows = normed.reshape(-1, normed.shape[-1])
    keys_out = jnp.dot(flat_rows, key_weight, preferred_element_type=jnp.float32).astype(jnp.bfloat16)
    values_out = jnp.dot(flat_rows, value_weight, preferred_element_type=jnp.float32).astype(jnp.bfloat16)
    return (keys_out.reshape(group_count, -1, keys_out.shape[-1]), values_out.reshape(group_count, -1, values_out.shape[-1]))

def attend(grouped, keys_in, values_in):
    group_count = grouped.shape[0]
    query_heads = grouped.astype(jnp.float32).reshape(group_count, SPAN, HEADS, DH)
    key_heads = keys_in.astype(jnp.float32).reshape(group_count, -1, HEADS, DH)
    value_heads = values_in.astype(jnp.float32).reshape(group_count, -1, HEADS, DH)
    scores = jnp.einsum('gqhd,gkhd->ghqk', query_heads, key_heads) * (1.0 / math.sqrt(DH))
    row_max = lax.optimization_barrier(jnp.max(scores, axis=-1, keepdims=True))
    expo = jnp.exp(scores - row_max)
    probs_low = (expo / lax.optimization_barrier(jnp.sum(expo, axis=-1, keepdims=True))).astype(jnp.bfloat16)
    mixed = jnp.einsum('ghqk,gkhd->gqhd', probs_low.astype(jnp.float32), value_heads)
    return mixed.reshape(group_count * SPAN, HEADS * DH).astype(jnp.bfloat16)

def reference(queries, database, enc_gain, key_weight, value_weight, ret_shard, ret_row):
    row_ids = (ret_shard * DB_DEV + ret_row).astype(jnp.int32)
    row_ids = jnp.concatenate([jnp.zeros((1, NBRS), jnp.int32), row_ids], axis=0)
    blocks = SPANS // CH_DEV
    token_count = CH_DEV * SPAN

    def one_block(block_index):
        start = (block_index * CH_DEV).astype(jnp.int32)
        block_ids = lax.dynamic_slice_in_dim(row_ids, start, CH_DEV + 1, 0)
        nbr_rows = database[block_ids]
        keys_in, values_in = encode(nbr_rows, enc_gain, key_weight, value_weight)
        present = (jnp.arange(CH_DEV + 1, dtype=jnp.int32) + block_index > 0).astype(keys_in.dtype)[:, None, None]
        keys_in = keys_in * present
        values_in = values_in * present
        block_queries = lax.dynamic_slice_in_dim(queries, (block_index * token_count).astype(jnp.int32), token_count, 0)
        padded = jnp.concatenate([jnp.zeros((1, HEADS * DH), queries.dtype), block_queries, jnp.zeros((SPAN - 1, HEADS * DH), queries.dtype)], axis=0)
        grouped = padded.reshape(CH_DEV + 1, SPAN, HEADS * DH)
        return attend(grouped, keys_in, values_in)[1:1 + token_count]
    result = lax.map(one_block, jnp.arange(blocks, dtype=jnp.int32))
    return result.reshape(TOKENS, HEADS * DH)
```

```python
import math

import jax
import jax.numpy as jnp
from jax import lax
from jax.sharding import PartitionSpec as P

HEADS = 16
DH = 128
SPAN = 64


eps_norm = 1e-06


def from_behind(block, axis, distance):
    devices = range(lax.axis_size(axis))
    route = [(i - distance, i) for i in devices if i - distance in devices]
    return lax.ppermute(block, axis, route)


def normalize(nbr_rows, enc_gain):
    widened = nbr_rows.astype(jnp.float32)
    mean_square = jnp.mean(widened * widened, axis=-1, keepdims=True)
    return (widened * lax.rsqrt(mean_square + eps_norm) * enc_gain).astype(jnp.bfloat16)


def project(nbr_rows, enc_gain, key_weight, value_weight):
    group_count = nbr_rows.shape[0]
    normed = normalize(nbr_rows, enc_gain)
    flat_rows = normed.reshape(-1, normed.shape[-1])
    key_part = jnp.dot(
        flat_rows,
        lax.all_gather(key_weight, "dp", axis=1, tiled=True),
        preferred_element_type=jnp.float32,
    )
    value_part = jnp.dot(
        flat_rows,
        lax.all_gather(value_weight, "dp", axis=1, tiled=True),
        preferred_element_type=jnp.float32,
    )
    keys_out = key_part.astype(jnp.bfloat16)
    values_out = value_part.astype(jnp.bfloat16)
    return (
        keys_out.reshape(group_count, -1, keys_out.shape[-1]),
        values_out.reshape(group_count, -1, values_out.shape[-1]),
    )


def attend(grouped, keys_in, values_in):
    group_count = grouped.shape[0]
    query_heads = grouped.reshape(group_count, SPAN, HEADS, DH)
    key_heads = keys_in.reshape(group_count, -1, HEADS, DH)
    value_heads = values_in.reshape(group_count, -1, HEADS, DH)
    scores = jnp.einsum(
        "gqhd,gkhd->ghqk", query_heads, key_heads, preferred_element_type=jnp.float32
    ) * (1.0 / math.sqrt(DH))
    row_max = jnp.max(scores, axis=-1, keepdims=True)
    expo = jnp.exp(scores - row_max)
    probs_low = (expo / jnp.sum(expo, axis=-1, keepdims=True)).astype(jnp.bfloat16)
    mixed = jnp.einsum(
        "ghqk,gkhd->gqhd", probs_low, value_heads, preferred_element_type=jnp.float32
    )
    return mixed.reshape(group_count * SPAN, HEADS * DH).astype(jnp.bfloat16)


def body(queries, database, enc_gain, key_weight, value_weight, ret_shard, ret_row):
    spans = ret_shard.shape[0]
    nbr_count = ret_shard.shape[1]
    owners = lax.axis_size("seq")
    capacity = max(2, min(spans, 2 * spans * nbr_count // owners))
    requests = spans * nbr_count
    length = database.shape[1]
    enc_width = database.shape[2]
    shard_flat = ret_shard.reshape(requests)
    row_flat = ret_row.reshape(requests)
    order = jnp.arange(requests, dtype=jnp.int32)
    same_owner = shard_flat[:, None] == shard_flat[None, :]
    earlier = order[None, :] < order[:, None]
    slot_rank = jnp.sum(jnp.logical_and(same_owner, earlier), axis=1)
    owner_ids = jnp.arange(owners, dtype=jnp.int32)
    slot_ids = jnp.arange(capacity, dtype=jnp.int32)
    matches = jnp.logical_and(
        shard_flat[None, None, :] == owner_ids[:, None, None],
        slot_rank[None, None, :] == slot_ids[None, :, None],
    )
    wanted = jnp.sum(jnp.where(matches, row_flat[None, None, :] + 1, 0), axis=2)
    asked_rows = lax.all_to_all(wanted, "seq", split_axis=0, concat_axis=0, tiled=True)
    filled = asked_rows.reshape(-1) > 0
    picked = jnp.take(database, jnp.maximum(asked_rows.reshape(-1) - 1, 0), axis=0)
    picked = jnp.where(filled[:, None, None], picked, jnp.zeros((), picked.dtype))
    reply_rows = picked.reshape(owners, capacity, length, enc_width)
    arrived = lax.all_to_all(reply_rows, "seq", split_axis=0, concat_axis=0, tiled=True)
    arrived = arrived.reshape(owners * capacity, length, enc_width)
    fetched = jnp.take(arrived, shard_flat * capacity + slot_rank, axis=0).reshape(
        spans, nbr_count, length, enc_width
    )
    prior_rows = from_behind(fetched[-1:], ("dp", "seq"), 1)
    keys_own, values_own = project(fetched, enc_gain, key_weight, value_weight)
    keys_prior, values_prior = project(prior_rows, enc_gain, key_weight, value_weight)
    keys_all = jnp.concatenate([keys_prior, keys_own], axis=0)
    values_all = jnp.concatenate([values_prior, values_own], axis=0)
    token_count = queries.shape[0]
    columns = queries.shape[1]
    padded = jnp.concatenate(
        [
            jnp.zeros((1, columns), queries.dtype),
            queries,
            jnp.zeros((SPAN - 1, columns), queries.dtype),
        ],
        axis=0,
    )
    grouped = padded.reshape(spans + 1, SPAN, columns)
    return attend(grouped, keys_all, values_all)[1 : 1 + token_count]


def solution(mesh):
    return jax.shard_map(
        body,
        mesh=mesh,
        in_specs=(
            P(("dp", "seq"), None),
            P("seq", None, None),
            P(),
            P(None, "dp"),
            P(None, "dp"),
            P(("dp", "seq"), None),
            P(("dp", "seq"), None),
        ),
        out_specs=P(("dp", "seq"), None),
        check_vma=False,
    )
```

```python
import functools
import math

import jax
import jax.numpy as jnp
from jax import lax
from jax.experimental import pallas as pl
from jax.experimental.pallas import tpu as pltpu
from jax.sharding import PartitionSpec as P

MESH = pl.DeviceIdType.MESH

HEADS = 16
DH = 128
SPAN = 64


eps_norm = 1e-06


def from_behind(block, axis, distance):
    devices = range(lax.axis_size(axis))
    route = [(i - distance, i) for i in devices if i - distance in devices]
    return lax.ppermute(block, axis, route)


def gathered_rows(ids, table_ref, length):
    shape = (2 * length, 128)
    sub = lax.broadcasted_iota(jnp.int32, shape, 0)
    lane = lax.broadcasted_iota(jnp.int32, shape, 1)
    sel = jnp.where(
        sub < length, jnp.broadcast_to(ids[0:1, :], shape), jnp.broadcast_to(ids[1:2, :], shape)
    )
    total = jnp.zeros((2 * length, table_ref.shape[1]), jnp.float32)
    for h in range(table_ref.shape[0] // 128):
        col = lane + h * 128
        hit = jnp.logical_and(col // length == sel, col % length == sub % length)
        total += jnp.dot(
            hit.astype(table_ref.dtype),
            table_ref[h * 128 : (h + 1) * 128, :],
            preferred_element_type=jnp.float32,
        )
    return total.astype(table_ref.dtype)


def fetch_kernel(length, wanted_ref, table_ref, out_ref, asked, outgoing, req_send, req_recv, rep_send, rep_recv):
    n = wanted_ref.shape[0]
    me = lax.axis_index("seq")
    dp = lax.axis_index("dp")

    def request(peer, slot):
        return pltpu.make_async_remote_copy(
            wanted_ref.at[peer], asked.at[slot], req_send.at[peer], req_recv.at[slot],
            device_id=(dp, peer), device_id_type=MESH,
        )

    def reply(peer, slot):
        return pltpu.make_async_remote_copy(
            outgoing.at[peer], out_ref.at[slot], rep_send.at[peer], rep_recv.at[slot],
            device_id=(dp, peer), device_id_type=MESH,
        )

    barrier = pltpu.get_barrier_semaphore()

    def greet(k, carry):
        pl.semaphore_signal(barrier, inc=1, device_id=(dp, lax.rem(me + k, n)), device_id_type=MESH)
        return carry

    lax.fori_loop(1, n, greet, 0)
    pl.semaphore_wait(barrier, n - 1)

    def ask(k, carry):
        request(lax.rem(me + k, n), me).start()
        return carry

    lax.fori_loop(1, n, ask, 0)
    out_ref[me] = gathered_rows(wanted_ref[me], table_ref, length)

    def serve(k, carry):
        source = lax.rem(me + n - k, n)
        request(source, source).wait_recv()
        outgoing[source] = gathered_rows(asked[source], table_ref, length)
        reply(source, me).start()
        return carry

    lax.fori_loop(1, n, serve, 0)

    def finish(k, carry):
        peer = lax.rem(me + k, n)
        request(peer, me).wait_send()
        reply(peer, me).wait_send()
        reply(peer, peer).wait_recv()
        return carry

    lax.fori_loop(1, n, finish, 0)


def fetch(wanted, table, length):
    n = wanted.shape[0]
    width = table.shape[1]
    return pl.pallas_call(
        functools.partial(fetch_kernel, length),
        out_shape=jax.ShapeDtypeStruct((n, 2 * length, width), table.dtype),
        in_specs=[pl.BlockSpec(memory_space=pltpu.VMEM)] * 2,
        out_specs=pl.BlockSpec(memory_space=pltpu.VMEM),
        scratch_shapes=[
            pltpu.VMEM(wanted.shape, jnp.int32),
            pltpu.VMEM((n, 2 * length, width), table.dtype),
            pltpu.SemaphoreType.DMA((n,)),
            pltpu.SemaphoreType.DMA((n,)),
            pltpu.SemaphoreType.DMA((n,)),
            pltpu.SemaphoreType.DMA((n,)),
        ],
        compiler_params=pltpu.CompilerParams(collective_id=0, has_side_effects=True),
    )(wanted, table)


def normalize(nbr_rows, enc_gain):
    widened = nbr_rows.astype(jnp.float32)
    mean_square = jnp.mean(widened * widened, axis=-1, keepdims=True)
    return (widened * lax.rsqrt(mean_square + eps_norm) * enc_gain).astype(jnp.bfloat16)


def project(nbr_rows, enc_gain, key_weight, value_weight):
    group_count = nbr_rows.shape[0]
    normed = normalize(nbr_rows, enc_gain)
    flat_rows = normed.reshape(-1, normed.shape[-1])
    key_part = jnp.dot(
        flat_rows,
        lax.all_gather(key_weight, "dp", axis=1, tiled=True),
        preferred_element_type=jnp.float32,
    )
    value_part = jnp.dot(
        flat_rows,
        lax.all_gather(value_weight, "dp", axis=1, tiled=True),
        preferred_element_type=jnp.float32,
    )
    keys_out = key_part.astype(jnp.bfloat16)
    values_out = value_part.astype(jnp.bfloat16)
    return (
        keys_out.reshape(group_count, -1, keys_out.shape[-1]),
        values_out.reshape(group_count, -1, values_out.shape[-1]),
    )


def attend(grouped, keys_in, values_in):
    group_count = grouped.shape[0]
    query_heads = grouped.reshape(group_count, SPAN, HEADS, DH)
    key_heads = keys_in.reshape(group_count, -1, HEADS, DH)
    value_heads = values_in.reshape(group_count, -1, HEADS, DH)
    scores = jnp.einsum(
        "gqhd,gkhd->ghqk", query_heads, key_heads, preferred_element_type=jnp.float32
    ) * (1.0 / math.sqrt(DH))
    row_max = jnp.max(scores, axis=-1, keepdims=True)
    expo = jnp.exp(scores - row_max)
    probs_low = (expo / jnp.sum(expo, axis=-1, keepdims=True)).astype(jnp.bfloat16)
    mixed = jnp.einsum(
        "ghqk,gkhd->gqhd", probs_low, value_heads, preferred_element_type=jnp.float32
    )
    return mixed.reshape(group_count * SPAN, HEADS * DH).astype(jnp.bfloat16)


def body(queries, database, enc_gain, key_weight, value_weight, ret_shard, ret_row):
    spans = ret_shard.shape[0]
    nbr_count = ret_shard.shape[1]
    owners = lax.axis_size("seq")
    capacity = max(2, min(spans, 2 * spans * nbr_count // owners))
    requests = spans * nbr_count
    length = database.shape[1]
    enc_width = database.shape[2]
    shard_flat = ret_shard.reshape(requests)
    row_flat = ret_row.reshape(requests)
    order = jnp.arange(requests, dtype=jnp.int32)
    same_owner = shard_flat[:, None] == shard_flat[None, :]
    earlier = order[None, :] < order[:, None]
    slot_rank = jnp.sum(jnp.logical_and(same_owner, earlier), axis=1)
    owner_ids = jnp.arange(owners, dtype=jnp.int32)
    slot_ids = jnp.arange(capacity, dtype=jnp.int32)
    matches = jnp.logical_and(
        shard_flat[None, None, :] == owner_ids[:, None, None],
        slot_rank[None, None, :] == slot_ids[None, :, None],
    )
    wanted = jnp.sum(jnp.where(matches, row_flat[None, None, :] + 1, 0), axis=2) - 1
    wanted = jnp.broadcast_to(wanted[:, :, None], (owners, capacity, 128))
    wanted = jnp.pad(wanted, ((0, 0), (0, 8 - capacity), (0, 0)), constant_values=-1)
    table = database.reshape(database.shape[0] * length, enc_width)
    arrived = fetch(wanted, table, length)
    arrived = arrived.reshape(owners * capacity, length, enc_width)
    fetched = jnp.take(arrived, shard_flat * capacity + slot_rank, axis=0).reshape(
        spans, nbr_count, length, enc_width
    )
    prior_rows = from_behind(fetched[-1:], ("dp", "seq"), 1)
    keys_own, values_own = project(fetched, enc_gain, key_weight, value_weight)
    keys_prior, values_prior = project(prior_rows, enc_gain, key_weight, value_weight)
    keys_all = jnp.concatenate([keys_prior, keys_own], axis=0)
    values_all = jnp.concatenate([values_prior, values_own], axis=0)
    token_count = queries.shape[0]
    columns = queries.shape[1]
    padded = jnp.concatenate(
        [
            jnp.zeros((1, columns), queries.dtype),
            queries,
            jnp.zeros((SPAN - 1, columns), queries.dtype),
        ],
        axis=0,
    )
    grouped = padded.reshape(spans + 1, SPAN, columns)
    return attend(grouped, keys_all, values_all)[1 : 1 + token_count]


def solution(mesh):
    return jax.shard_map(
        body,
        mesh=mesh,
        in_specs=(
            P(("dp", "seq"), None),
            P("seq", None, None),
            P(),
            P(None, "dp"),
            P(None, "dp"),
            P(("dp", "seq"), None),
            P(("dp", "seq"), None),
        ),
        out_specs=P(("dp", "seq"), None),
        check_vma=False,
    )
```

```python
import functools
import math

import jax
import jax.numpy as jnp
from jax import lax
from jax.experimental import pallas as pl
from jax.experimental.pallas import tpu as pltpu
from jax.sharding import PartitionSpec as P

MESH = pl.DeviceIdType.MESH

HEADS = 16
DH = 128
SPAN = 64


eps_norm = 1e-06


def from_behind(block, axis, distance):
    devices = range(lax.axis_size(axis))
    route = [(i - distance, i) for i in devices if i - distance in devices]
    return lax.ppermute(block, axis, route)


def gathered_rows(ids_list, table_ref, length):
    pieces = []
    for ids in ids_list:
        for slot in range(2):
            pieces.append(jnp.broadcast_to(ids[slot : slot + 1, :], (length, 128)))
    sel = jnp.concatenate(pieces, axis=0)
    shape = sel.shape
    sub = lax.broadcasted_iota(jnp.int32, shape, 0)
    lane = lax.broadcasted_iota(jnp.int32, shape, 1)
    total = jnp.zeros((shape[0], table_ref.shape[1]), jnp.float32)
    for h in range(table_ref.shape[0] // 128):
        col = lane + h * 128
        hit = jnp.logical_and(col // length == sel, col % length == sub % length)
        total += jnp.dot(
            hit.astype(table_ref.dtype),
            table_ref[h * 128 : (h + 1) * 128, :],
            preferred_element_type=jnp.float32,
        )
    return total.astype(table_ref.dtype)


def fetch_kernel(length, group, wanted_ref, table_ref, out_ref, asked, outgoing, req_send, req_recv, rep_send, rep_recv):
    n = wanted_ref.shape[0]
    me = lax.axis_index("seq")
    dp = lax.axis_index("dp")

    def request(peer, slot):
        return pltpu.make_async_remote_copy(
            wanted_ref.at[peer], asked.at[slot], req_send.at[peer], req_recv.at[slot],
            device_id=(dp, peer), device_id_type=MESH,
        )

    def reply(step, peer, slot):
        return pltpu.make_async_remote_copy(
            outgoing.at[step], out_ref.at[slot], rep_send.at[step], rep_recv.at[slot],
            device_id=(dp, peer), device_id_type=MESH,
        )

    barrier = pltpu.get_barrier_semaphore()

    def greet(k, carry):
        pl.semaphore_signal(barrier, inc=1, device_id=(dp, lax.rem(me + k, n)), device_id_type=MESH)
        return carry

    lax.fori_loop(1, n, greet, 0)
    pl.semaphore_wait(barrier, n - 1)

    def ask(k, carry):
        request(lax.rem(me + k, n), me).start()
        return carry

    lax.fori_loop(1, n, ask, 0)
    asked[me] = wanted_ref[me]

    def serve(c, carry):
        ids_list = []
        for j in range(group):
            k = c * group + j
            source = lax.rem(me + n - k, n)

            @pl.when(k > 0)
            def _():
                request(source, source).wait_recv()

            ids_list.append(asked[source])
        rows = gathered_rows(ids_list, table_ref, length)
        outgoing[pl.ds(c * group, group)] = rows.reshape(group, 2 * length, rows.shape[-1])
        for j in range(group):
            k = c * group + j
            source = lax.rem(me + n - k, n)

            @pl.when(k == 0)
            def _():
                out_ref[me] = outgoing[k]

            @pl.when(k > 0)
            def _():
                reply(k, source, me).start()

        return carry

    lax.fori_loop(0, n // group, serve, 0)

    def finish(k, carry):
        peer = lax.rem(me + k, n)
        request(peer, me).wait_send()
        reply(k, lax.rem(me + n - k, n), me).wait_send()
        reply(k, peer, peer).wait_recv()
        return carry

    lax.fori_loop(1, n, finish, 0)


def fetch(wanted, table, length):
    n = wanted.shape[0]
    width = table.shape[1]
    return pl.pallas_call(
        functools.partial(fetch_kernel, length, math.gcd(8, n)),
        out_shape=jax.ShapeDtypeStruct((n, 2 * length, width), table.dtype),
        in_specs=[pl.BlockSpec(memory_space=pltpu.VMEM)] * 2,
        out_specs=pl.BlockSpec(memory_space=pltpu.VMEM),
        scratch_shapes=[
            pltpu.VMEM(wanted.shape, jnp.int32),
            pltpu.VMEM((n, 2 * length, width), table.dtype),
            pltpu.SemaphoreType.DMA((n,)),
            pltpu.SemaphoreType.DMA((n,)),
            pltpu.SemaphoreType.DMA((n,)),
            pltpu.SemaphoreType.DMA((n,)),
        ],
        compiler_params=pltpu.CompilerParams(collective_id=0, has_side_effects=True),
    )(wanted, table)


def normalize(nbr_rows, enc_gain):
    widened = nbr_rows.astype(jnp.float32)
    mean_square = jnp.mean(widened * widened, axis=-1, keepdims=True)
    return (widened * lax.rsqrt(mean_square + eps_norm) * enc_gain).astype(jnp.bfloat16)


def project(nbr_rows, enc_gain, key_weight, value_weight):
    group_count = nbr_rows.shape[0]
    normed = normalize(nbr_rows, enc_gain)
    flat_rows = normed.reshape(-1, normed.shape[-1])
    key_part = jnp.dot(
        flat_rows,
        lax.all_gather(key_weight, "dp", axis=1, tiled=True),
        preferred_element_type=jnp.float32,
    )
    value_part = jnp.dot(
        flat_rows,
        lax.all_gather(value_weight, "dp", axis=1, tiled=True),
        preferred_element_type=jnp.float32,
    )
    keys_out = key_part.astype(jnp.bfloat16)
    values_out = value_part.astype(jnp.bfloat16)
    return (
        keys_out.reshape(group_count, -1, keys_out.shape[-1]),
        values_out.reshape(group_count, -1, values_out.shape[-1]),
    )


def attend(grouped, keys_in, values_in):
    group_count = grouped.shape[0]
    query_heads = grouped.reshape(group_count, SPAN, HEADS, DH)
    key_heads = keys_in.reshape(group_count, -1, HEADS, DH)
    value_heads = values_in.reshape(group_count, -1, HEADS, DH)
    scores = jnp.einsum(
        "gqhd,gkhd->ghqk", query_heads, key_heads, preferred_element_type=jnp.float32
    ) * (1.0 / math.sqrt(DH))
    row_max = jnp.max(scores, axis=-1, keepdims=True)
    expo = jnp.exp(scores - row_max)
    probs_low = (expo / jnp.sum(expo, axis=-1, keepdims=True)).astype(jnp.bfloat16)
    mixed = jnp.einsum(
        "ghqk,gkhd->gqhd", probs_low, value_heads, preferred_element_type=jnp.float32
    )
    return mixed.reshape(group_count * SPAN, HEADS * DH).astype(jnp.bfloat16)


def body(queries, database, enc_gain, key_weight, value_weight, ret_shard, ret_row):
    spans = ret_shard.shape[0]
    nbr_count = ret_shard.shape[1]
    owners = lax.axis_size("seq")
    capacity = max(2, min(spans, 2 * spans * nbr_count // owners))
    requests = spans * nbr_count
    length = database.shape[1]
    enc_width = database.shape[2]
    shard_flat = ret_shard.reshape(requests)
    row_flat = ret_row.reshape(requests)
    order = jnp.arange(requests, dtype=jnp.int32)
    same_owner = shard_flat[:, None] == shard_flat[None, :]
    earlier = order[None, :] < order[:, None]
    slot_rank = jnp.sum(jnp.logical_and(same_owner, earlier), axis=1)
    owner_ids = jnp.arange(owners, dtype=jnp.int32)
    slot_ids = jnp.arange(capacity, dtype=jnp.int32)
    matches = jnp.logical_and(
        shard_flat[None, None, :] == owner_ids[:, None, None],
        slot_rank[None, None, :] == slot_ids[None, :, None],
    )
    wanted = jnp.sum(jnp.where(matches, row_flat[None, None, :] + 1, 0), axis=2) - 1
    wanted = jnp.broadcast_to(wanted[:, :, None], (owners, capacity, 128))
    wanted = jnp.pad(wanted, ((0, 0), (0, 8 - capacity), (0, 0)), constant_values=-1)
    table = database.reshape(database.shape[0] * length, enc_width)
    arrived = fetch(wanted, table, length)
    arrived = arrived.reshape(owners * capacity, length, enc_width)
    fetched = jnp.take(arrived, shard_flat * capacity + slot_rank, axis=0).reshape(
        spans, nbr_count, length, enc_width
    )
    prior_rows = from_behind(fetched[-1:], ("dp", "seq"), 1)
    keys_own, values_own = project(fetched, enc_gain, key_weight, value_weight)
    keys_prior, values_prior = project(prior_rows, enc_gain, key_weight, value_weight)
    keys_all = jnp.concatenate([keys_prior, keys_own], axis=0)
    values_all = jnp.concatenate([values_prior, values_own], axis=0)
    token_count = queries.shape[0]
    columns = queries.shape[1]
    padded = jnp.concatenate(
        [
            jnp.zeros((1, columns), queries.dtype),
            queries,
            jnp.zeros((SPAN - 1, columns), queries.dtype),
        ],
        axis=0,
    )
    grouped = padded.reshape(spans + 1, SPAN, columns)
    return attend(grouped, keys_all, values_all)[1 : 1 + token_count]


def solution(mesh):
    return jax.shard_map(
        body,
        mesh=mesh,
        in_specs=(
            P(("dp", "seq"), None),
            P("seq", None, None),
            P(),
            P(None, "dp"),
            P(None, "dp"),
            P(("dp", "seq"), None),
            P(("dp", "seq"), None),
        ),
        out_specs=P(("dp", "seq"), None),
        check_vma=False,
    )
```

```python
import functools
import math

import jax
import jax.numpy as jnp
from jax import lax
from jax.experimental import pallas as pl
from jax.experimental.pallas import tpu as pltpu
from jax.sharding import PartitionSpec as P

MESH = pl.DeviceIdType.MESH

HEADS = 16
DH = 128
SPAN = 64


eps_norm = 1e-06


def from_behind(block, axis, distance):
    devices = range(lax.axis_size(axis))
    route = [(i - distance, i) for i in devices if i - distance in devices]
    return lax.ppermute(block, axis, route)


def gathered_rows(ids_list, table_ref, length):
    pieces = []
    for ids in ids_list:
        for slot in range(2):
            pieces.append(jnp.broadcast_to(ids[slot : slot + 1, :], (length, 128)))
    sel = jnp.concatenate(pieces, axis=0)
    shape = sel.shape
    sub = lax.broadcasted_iota(jnp.int32, shape, 0)
    lane = lax.broadcasted_iota(jnp.int32, shape, 1)
    total = jnp.zeros((shape[0], table_ref.shape[1]), jnp.float32)
    for h in range(table_ref.shape[0] // 128):
        col = lane + h * 128
        hit = jnp.logical_and(col // length == sel, col % length == sub % length)
        total += jnp.dot(
            hit.astype(table_ref.dtype),
            table_ref[h * 128 : (h + 1) * 128, :],
            preferred_element_type=jnp.float32,
        )
    return total.astype(table_ref.dtype)


def torus_step(k, across, sign):
    i = k // across
    j = lax.rem(k, across)
    dz = sign * ((i + 1) // 2) * (2 * lax.rem(i, 2) - 1)
    dy = sign * ((j + 1) // 2) * (2 * lax.rem(j, 2) - 1)
    return dy, dz


def fetch_kernel(length, group, wanted_ref, table_ref, out_ref, asked, outgoing, req_send, req_recv, rep_send, rep_recv):
    n = wanted_ref.shape[0]
    me = lax.axis_index("seq")
    dp = lax.axis_index("dp")
    across = math.gcd(4, n)
    depth = n // across

    def peer_of(k, sign):
        dy, dz = torus_step(k, across, sign)
        y = lax.rem(me, across)
        z = me // across
        return lax.rem(z + dz + depth, depth) * across + lax.rem(y + dy + across, across)

    def request(peer, slot):
        return pltpu.make_async_remote_copy(
            wanted_ref.at[peer], asked.at[slot], req_send.at[peer], req_recv.at[slot],
            device_id=(dp, peer), device_id_type=MESH,
        )

    def reply(step, peer, slot):
        return pltpu.make_async_remote_copy(
            outgoing.at[step], out_ref.at[slot], rep_send.at[step], rep_recv.at[slot],
            device_id=(dp, peer), device_id_type=MESH,
        )

    barrier = pltpu.get_barrier_semaphore()

    def greet(k, carry):
        pl.semaphore_signal(barrier, inc=1, device_id=(dp, lax.rem(me + k, n)), device_id_type=MESH)
        return carry

    lax.fori_loop(1, n, greet, 0)
    pl.semaphore_wait(barrier, n - 1)

    def ask(k, carry):
        request(peer_of(k, 1), me).start()
        return carry

    lax.fori_loop(1, n, ask, 0)
    asked[me] = wanted_ref[me]

    def serve(c, carry):
        ids_list = []
        for j in range(group):
            k = c * group + j
            source = peer_of(k, -1)

            @pl.when(k > 0)
            def _():
                request(source, source).wait_recv()

            ids_list.append(asked[source])
        rows = gathered_rows(ids_list, table_ref, length)
        outgoing[pl.ds(c * group, group)] = rows.reshape(group, 2 * length, rows.shape[-1])
        for j in range(group):
            k = c * group + j
            source = peer_of(k, -1)

            @pl.when(k == 0)
            def _():
                out_ref[me] = outgoing[k]

            @pl.when(k > 0)
            def _():
                reply(k, source, me).start()

        return carry

    lax.fori_loop(0, n // group, serve, 0)

    def finish(k, carry):
        peer = peer_of(k, 1)
        request(peer, me).wait_send()
        reply(k, peer_of(k, -1), me).wait_send()
        reply(k, peer, peer).wait_recv()
        return carry

    lax.fori_loop(1, n, finish, 0)


def fetch(wanted, table, length):
    n = wanted.shape[0]
    width = table.shape[1]
    return pl.pallas_call(
        functools.partial(fetch_kernel, length, math.gcd(8, n)),
        out_shape=jax.ShapeDtypeStruct((n, 2 * length, width), table.dtype),
        in_specs=[pl.BlockSpec(memory_space=pltpu.VMEM)] * 2,
        out_specs=pl.BlockSpec(memory_space=pltpu.VMEM),
        scratch_shapes=[
            pltpu.VMEM(wanted.shape, jnp.int32),
            pltpu.VMEM((n, 2 * length, width), table.dtype),
            pltpu.SemaphoreType.DMA((n,)),
            pltpu.SemaphoreType.DMA((n,)),
            pltpu.SemaphoreType.DMA((n,)),
            pltpu.SemaphoreType.DMA((n,)),
        ],
        compiler_params=pltpu.CompilerParams(collective_id=0, has_side_effects=True),
    )(wanted, table)


def normalize(nbr_rows, enc_gain):
    widened = nbr_rows.astype(jnp.float32)
    mean_square = jnp.mean(widened * widened, axis=-1, keepdims=True)
    return (widened * lax.rsqrt(mean_square + eps_norm) * enc_gain).astype(jnp.bfloat16)


def project(nbr_rows, enc_gain, key_weight, value_weight):
    group_count = nbr_rows.shape[0]
    normed = normalize(nbr_rows, enc_gain)
    flat_rows = normed.reshape(-1, normed.shape[-1])
    key_part = jnp.dot(
        flat_rows,
        lax.all_gather(key_weight, "dp", axis=1, tiled=True),
        preferred_element_type=jnp.float32,
    )
    value_part = jnp.dot(
        flat_rows,
        lax.all_gather(value_weight, "dp", axis=1, tiled=True),
        preferred_element_type=jnp.float32,
    )
    keys_out = key_part.astype(jnp.bfloat16)
    values_out = value_part.astype(jnp.bfloat16)
    return (
        keys_out.reshape(group_count, -1, keys_out.shape[-1]),
        values_out.reshape(group_count, -1, values_out.shape[-1]),
    )


def attend(grouped, keys_in, values_in):
    group_count = grouped.shape[0]
    query_heads = grouped.reshape(group_count, SPAN, HEADS, DH)
    key_heads = keys_in.reshape(group_count, -1, HEADS, DH)
    value_heads = values_in.reshape(group_count, -1, HEADS, DH)
    scores = jnp.einsum(
        "gqhd,gkhd->ghqk", query_heads, key_heads, preferred_element_type=jnp.float32
    ) * (1.0 / math.sqrt(DH))
    row_max = jnp.max(scores, axis=-1, keepdims=True)
    expo = jnp.exp(scores - row_max)
    probs_low = (expo / jnp.sum(expo, axis=-1, keepdims=True)).astype(jnp.bfloat16)
    mixed = jnp.einsum(
        "ghqk,gkhd->gqhd", probs_low, value_heads, preferred_element_type=jnp.float32
    )
    return mixed.reshape(group_count * SPAN, HEADS * DH).astype(jnp.bfloat16)


def body(queries, database, enc_gain, key_weight, value_weight, ret_shard, ret_row):
    spans = ret_shard.shape[0]
    nbr_count = ret_shard.shape[1]
    owners = lax.axis_size("seq")
    capacity = max(2, min(spans, 2 * spans * nbr_count // owners))
    requests = spans * nbr_count
    length = database.shape[1]
    enc_width = database.shape[2]
    shard_flat = ret_shard.reshape(requests)
    row_flat = ret_row.reshape(requests)
    order = jnp.arange(requests, dtype=jnp.int32)
    same_owner = shard_flat[:, None] == shard_flat[None, :]
    earlier = order[None, :] < order[:, None]
    slot_rank = jnp.sum(jnp.logical_and(same_owner, earlier), axis=1)
    owner_ids = jnp.arange(owners, dtype=jnp.int32)
    slot_ids = jnp.arange(capacity, dtype=jnp.int32)
    matches = jnp.logical_and(
        shard_flat[None, None, :] == owner_ids[:, None, None],
        slot_rank[None, None, :] == slot_ids[None, :, None],
    )
    wanted = jnp.sum(jnp.where(matches, row_flat[None, None, :] + 1, 0), axis=2) - 1
    wanted = jnp.broadcast_to(wanted[:, :, None], (owners, capacity, 128))
    wanted = jnp.pad(wanted, ((0, 0), (0, 8 - capacity), (0, 0)), constant_values=-1)
    table = database.reshape(database.shape[0] * length, enc_width)
    arrived = fetch(wanted, table, length)
    arrived = arrived.reshape(owners * capacity, length, enc_width)
    fetched = jnp.take(arrived, shard_flat * capacity + slot_rank, axis=0).reshape(
        spans, nbr_count, length, enc_width
    )
    prior_rows = from_behind(fetched[-1:], ("dp", "seq"), 1)
    keys_own, values_own = project(fetched, enc_gain, key_weight, value_weight)
    keys_prior, values_prior = project(prior_rows, enc_gain, key_weight, value_weight)
    keys_all = jnp.concatenate([keys_prior, keys_own], axis=0)
    values_all = jnp.concatenate([values_prior, values_own], axis=0)
    token_count = queries.shape[0]
    columns = queries.shape[1]
    padded = jnp.concatenate(
        [
            jnp.zeros((1, columns), queries.dtype),
            queries,
            jnp.zeros((SPAN - 1, columns), queries.dtype),
        ],
        axis=0,
    )
    grouped = padded.reshape(spans + 1, SPAN, columns)
    return attend(grouped, keys_all, values_all)[1 : 1 + token_count]


def solution(mesh):
    return jax.shard_map(
        body,
        mesh=mesh,
        in_specs=(
            P(("dp", "seq"), None),
            P("seq", None, None),
            P(),
            P(None, "dp"),
            P(None, "dp"),
            P(("dp", "seq"), None),
            P(("dp", "seq"), None),
        ),
        out_specs=P(("dp", "seq"), None),
        check_vma=False,
    )
```

```python
import functools
import math

import jax
import jax.numpy as jnp
from jax import lax
from jax.experimental import pallas as pl
from jax.experimental.pallas import tpu as pltpu
from jax.sharding import PartitionSpec as P

MESH = pl.DeviceIdType.MESH

HEADS = 16
DH = 128
SPAN = 64


eps_norm = 1e-06


def from_behind(block, axis, distance):
    devices = range(lax.axis_size(axis))
    route = [(i - distance, i) for i in devices if i - distance in devices]
    return lax.ppermute(block, axis, route)


def gathered_rows(ids_list, table_ref, length):
    pieces = []
    for ids in ids_list:
        for slot in range(2):
            pieces.append(jnp.broadcast_to(ids[slot : slot + 1, :], (length, 128)))
    sel = jnp.concatenate(pieces, axis=0)
    shape = sel.shape
    sub = lax.broadcasted_iota(jnp.int32, shape, 0)
    lane = lax.broadcasted_iota(jnp.int32, shape, 1)
    total = jnp.zeros((shape[0], table_ref.shape[1]), jnp.float32)
    for h in range(table_ref.shape[0] // 128):
        col = lane + h * 128
        hit = jnp.logical_and(col // length == sel, col % length == sub % length)
        total += jnp.dot(
            hit.astype(table_ref.dtype),
            table_ref[h * 128 : (h + 1) * 128, :],
            preferred_element_type=jnp.float32,
        )
    return total.astype(table_ref.dtype)


def torus_step(k, across, sign):
    i = k // across
    j = lax.rem(k, across)
    dz = sign * ((i + 1) // 2) * (2 * lax.rem(i, 2) - 1)
    dy = sign * ((j + 1) // 2) * (2 * lax.rem(j, 2) - 1)
    return dy, dz


def fetch_kernel(
    length, group, wanted_ref, table_ref, wk_ref, wv_ref, out_ref, wk_out, wv_out,
    asked, outgoing, req_send, req_recv, rep_send, rep_recv, wk_send, wk_recv, wv_send, wv_recv, own_sem,
):
    n = wanted_ref.shape[0]
    nd = wk_out.shape[0]
    me = lax.axis_index("seq")
    dp = lax.axis_index("dp")
    across = math.gcd(4, n)
    depth = n // across

    def peer_of(k, sign):
        dy, dz = torus_step(k, across, sign)
        y = lax.rem(me, across)
        z = me // across
        return lax.rem(z + dz + depth, depth) * across + lax.rem(y + dy + across, across)

    def request(peer, slot):
        return pltpu.make_async_remote_copy(
            wanted_ref.at[peer], asked.at[slot], req_send.at[peer], req_recv.at[slot],
            device_id=(dp, peer), device_id_type=MESH,
        )

    def reply(step, peer, slot):
        return pltpu.make_async_remote_copy(
            outgoing.at[step], out_ref.at[slot], rep_send.at[step], rep_recv.at[slot],
            device_id=(dp, peer), device_id_type=MESH,
        )

    def weight(src, dst, send, recv, peer, slot):
        return pltpu.make_async_remote_copy(
            src, dst.at[slot], send.at[peer], recv.at[slot],
            device_id=(peer, me), device_id_type=MESH,
        )

    def weights(peer, slot):
        return (
            weight(wk_ref, wk_out, wk_send, wk_recv, peer, slot),
            weight(wv_ref, wv_out, wv_send, wv_recv, peer, slot),
        )

    own = (
        pltpu.make_async_copy(wk_ref, wk_out.at[dp], own_sem.at[0]),
        pltpu.make_async_copy(wv_ref, wv_out.at[dp], own_sem.at[1]),
    )

    barrier = pltpu.get_barrier_semaphore()

    def greet(k, carry):
        pl.semaphore_signal(barrier, inc=1, device_id=(dp, lax.rem(me + k, n)), device_id_type=MESH)
        return carry

    def greet_dp(k, carry):
        pl.semaphore_signal(barrier, inc=1, device_id=(lax.rem(dp + k, nd), me), device_id_type=MESH)
        return carry

    lax.fori_loop(1, n, greet, 0)
    lax.fori_loop(1, nd, greet_dp, 0)
    pl.semaphore_wait(barrier, n - 1 + nd - 1)

    def ask(k, carry):
        request(peer_of(k, 1), me).start()
        return carry

    lax.fori_loop(1, n, ask, 0)

    def share(k, carry):
        for copy in weights(lax.rem(dp + k, nd), dp):
            copy.start()
        return carry

    lax.fori_loop(1, nd, share, 0)
    for copy in own:
        copy.start()
    asked[me] = wanted_ref[me]

    def serve(c, carry):
        ids_list = []
        for j in range(group):
            k = c * group + j
            source = peer_of(k, -1)

            @pl.when(k > 0)
            def _():
                request(source, source).wait_recv()

            ids_list.append(asked[source])
        rows = gathered_rows(ids_list, table_ref, length)
        outgoing[pl.ds(c * group, group)] = rows.reshape(group, 2 * length, rows.shape[-1])
        for j in range(group):
            k = c * group + j
            source = peer_of(k, -1)

            @pl.when(k == 0)
            def _():
                out_ref[me] = outgoing[k]

            @pl.when(k > 0)
            def _():
                reply(k, source, me).start()

        return carry

    lax.fori_loop(0, n // group, serve, 0)

    def finish(k, carry):
        peer = peer_of(k, 1)
        request(peer, me).wait_send()
        reply(k, peer_of(k, -1), me).wait_send()
        reply(k, peer, peer).wait_recv()
        return carry

    lax.fori_loop(1, n, finish, 0)

    def gathered(k, carry):
        peer = lax.rem(dp + k, nd)
        for copy in weights(peer, dp):
            copy.wait_send()
        for copy in weights(peer, peer):
            copy.wait_recv()
        return carry

    lax.fori_loop(1, nd, gathered, 0)
    for copy in own:
        copy.wait()


def fetch(wanted, table, key_weight, value_weight, length, nd):
    n = wanted.shape[0]
    width = table.shape[1]
    vmem = pl.BlockSpec(memory_space=pltpu.VMEM)
    anywhere = pl.BlockSpec(memory_space=pl.ANY)
    return pl.pallas_call(
        functools.partial(fetch_kernel, length, math.gcd(8, n)),
        out_shape=(
            jax.ShapeDtypeStruct((n, 2 * length, width), table.dtype),
            jax.ShapeDtypeStruct((nd,) + key_weight.shape, key_weight.dtype),
            jax.ShapeDtypeStruct((nd,) + value_weight.shape, value_weight.dtype),
        ),
        in_specs=[vmem, vmem, anywhere, anywhere],
        out_specs=(vmem, anywhere, anywhere),
        scratch_shapes=[
            pltpu.VMEM(wanted.shape, jnp.int32),
            pltpu.VMEM((n, 2 * length, width), table.dtype),
            pltpu.SemaphoreType.DMA((n,)),
            pltpu.SemaphoreType.DMA((n,)),
            pltpu.SemaphoreType.DMA((n,)),
            pltpu.SemaphoreType.DMA((n,)),
            pltpu.SemaphoreType.DMA((nd,)),
            pltpu.SemaphoreType.DMA((nd,)),
            pltpu.SemaphoreType.DMA((nd,)),
            pltpu.SemaphoreType.DMA((nd,)),
            pltpu.SemaphoreType.DMA((2,)),
        ],
        compiler_params=pltpu.CompilerParams(collective_id=0, has_side_effects=True),
    )(wanted, table, key_weight, value_weight)


def normalize(nbr_rows, enc_gain):
    widened = nbr_rows.astype(jnp.float32)
    mean_square = jnp.mean(widened * widened, axis=-1, keepdims=True)
    return (widened * lax.rsqrt(mean_square + eps_norm) * enc_gain).astype(jnp.bfloat16)


def project(nbr_rows, enc_gain, key_weight, value_weight):
    group_count = nbr_rows.shape[0]
    normed = normalize(nbr_rows, enc_gain)
    flat_rows = normed.reshape(-1, normed.shape[-1])
    key_part = jnp.einsum(
        "td,idc->tic", flat_rows, key_weight, preferred_element_type=jnp.float32
    ).reshape(flat_rows.shape[0], -1)
    value_part = jnp.einsum(
        "td,idc->tic", flat_rows, value_weight, preferred_element_type=jnp.float32
    ).reshape(flat_rows.shape[0], -1)
    keys_out = key_part.astype(jnp.bfloat16)
    values_out = value_part.astype(jnp.bfloat16)
    return (
        keys_out.reshape(group_count, -1, keys_out.shape[-1]),
        values_out.reshape(group_count, -1, values_out.shape[-1]),
    )


def attend(grouped, keys_in, values_in):
    group_count = grouped.shape[0]
    query_heads = grouped.reshape(group_count, SPAN, HEADS, DH)
    key_heads = keys_in.reshape(group_count, -1, HEADS, DH)
    value_heads = values_in.reshape(group_count, -1, HEADS, DH)
    scores = jnp.einsum(
        "gqhd,gkhd->ghqk", query_heads, key_heads, preferred_element_type=jnp.float32
    ) * (1.0 / math.sqrt(DH))
    row_max = jnp.max(scores, axis=-1, keepdims=True)
    expo = jnp.exp(scores - row_max)
    probs_low = (expo / jnp.sum(expo, axis=-1, keepdims=True)).astype(jnp.bfloat16)
    mixed = jnp.einsum(
        "ghqk,gkhd->gqhd", probs_low, value_heads, preferred_element_type=jnp.float32
    )
    return mixed.reshape(group_count * SPAN, HEADS * DH).astype(jnp.bfloat16)


def body(queries, database, enc_gain, key_weight, value_weight, ret_shard, ret_row):
    spans = ret_shard.shape[0]
    nbr_count = ret_shard.shape[1]
    owners = lax.axis_size("seq")
    capacity = max(2, min(spans, 2 * spans * nbr_count // owners))
    requests = spans * nbr_count
    length = database.shape[1]
    enc_width = database.shape[2]
    shard_flat = ret_shard.reshape(requests)
    row_flat = ret_row.reshape(requests)
    order = jnp.arange(requests, dtype=jnp.int32)
    same_owner = shard_flat[:, None] == shard_flat[None, :]
    earlier = order[None, :] < order[:, None]
    slot_rank = jnp.sum(jnp.logical_and(same_owner, earlier), axis=1)
    owner_ids = jnp.arange(owners, dtype=jnp.int32)
    slot_ids = jnp.arange(capacity, dtype=jnp.int32)
    matches = jnp.logical_and(
        shard_flat[None, None, :] == owner_ids[:, None, None],
        slot_rank[None, None, :] == slot_ids[None, :, None],
    )
    wanted = jnp.sum(jnp.where(matches, row_flat[None, None, :] + 1, 0), axis=2) - 1
    wanted = jnp.broadcast_to(wanted[:, :, None], (owners, capacity, 128))
    wanted = jnp.pad(wanted, ((0, 0), (0, 8 - capacity), (0, 0)), constant_values=-1)
    table = database.reshape(database.shape[0] * length, enc_width)
    arrived, key_weight, value_weight = fetch(
        wanted, table, key_weight, value_weight, length, lax.axis_size("dp")
    )
    arrived = arrived.reshape(owners * capacity, length, enc_width)
    fetched = jnp.take(arrived, shard_flat * capacity + slot_rank, axis=0).reshape(
        spans, nbr_count, length, enc_width
    )
    prior_rows = from_behind(fetched[-1:], ("dp", "seq"), 1)
    keys_own, values_own = project(fetched, enc_gain, key_weight, value_weight)
    keys_prior, values_prior = project(prior_rows, enc_gain, key_weight, value_weight)
    keys_all = jnp.concatenate([keys_prior, keys_own], axis=0)
    values_all = jnp.concatenate([values_prior, values_own], axis=0)
    token_count = queries.shape[0]
    columns = queries.shape[1]
    padded = jnp.concatenate(
        [
            jnp.zeros((1, columns), queries.dtype),
            queries,
            jnp.zeros((SPAN - 1, columns), queries.dtype),
        ],
        axis=0,
    )
    grouped = padded.reshape(spans + 1, SPAN, columns)
    return attend(grouped, keys_all, values_all)[1 : 1 + token_count]


def solution(mesh):
    return jax.shard_map(
        body,
        mesh=mesh,
        in_specs=(
            P(("dp", "seq"), None),
            P("seq", None, None),
            P(),
            P(None, "dp"),
            P(None, "dp"),
            P(("dp", "seq"), None),
            P(("dp", "seq"), None),
        ),
        out_specs=P(("dp", "seq"), None),
        check_vma=False,
    )
```

```python
import functools
import math

import jax
import jax.numpy as jnp
from jax import lax
from jax.experimental import pallas as pl
from jax.experimental.pallas import tpu as pltpu
from jax.sharding import PartitionSpec as P

MESH = pl.DeviceIdType.MESH

HEADS = 16
DH = 128
SPAN = 64


eps_norm = 1e-06


def from_behind(block, axis, distance):
    devices = range(lax.axis_size(axis))
    route = [(i - distance, i) for i in devices if i - distance in devices]
    return lax.ppermute(block, axis, route)


def gathered_rows(ids_list, table_ref, length):
    pieces = []
    for ids in ids_list:
        for slot in range(2):
            pieces.append(jnp.broadcast_to(ids[slot : slot + 1, :], (length, 128)))
    sel = jnp.concatenate(pieces, axis=0)
    shape = sel.shape
    sub = lax.broadcasted_iota(jnp.int32, shape, 0)
    lane = lax.broadcasted_iota(jnp.int32, shape, 1)
    total = jnp.zeros((shape[0], table_ref.shape[1]), jnp.float32)
    for h in range(table_ref.shape[0] // 128):
        col = lane + h * 128
        hit = jnp.logical_and(col // length == sel, col % length == sub % length)
        total += jnp.dot(
            hit.astype(table_ref.dtype),
            table_ref[h * 128 : (h + 1) * 128, :],
            preferred_element_type=jnp.float32,
        )
    return total.astype(table_ref.dtype)


def torus_step(k, across, sign):
    i = k // across
    j = lax.rem(k, across)
    dz = sign * ((i + 1) // 2) * (2 * lax.rem(i, 2) - 1)
    dy = sign * ((j + 1) // 2) * (2 * lax.rem(j, 2) - 1)
    return dy, dz


def fetch_kernel(
    length, group, wanted_ref, table_ref, wk_ref, wv_ref, out_ref, wk_out, wv_out,
    asked, outgoing, req_send, req_recv, rep_send, rep_recv, wk_send, wk_recv, wv_send, wv_recv, own_sem,
):
    n = wanted_ref.shape[0]
    nd = wk_out.shape[1] // wk_ref.shape[1]
    me = lax.axis_index("seq")
    dp = lax.axis_index("dp")
    across = math.gcd(4, n)
    depth = n // across

    def peer_of(k, sign):
        dy, dz = torus_step(k, across, sign)
        y = lax.rem(me, across)
        z = me // across
        return lax.rem(z + dz + depth, depth) * across + lax.rem(y + dy + across, across)

    def request(peer, slot):
        return pltpu.make_async_remote_copy(
            wanted_ref.at[peer], asked.at[slot], req_send.at[peer], req_recv.at[slot],
            device_id=(dp, peer), device_id_type=MESH,
        )

    def reply(step, peer, slot):
        return pltpu.make_async_remote_copy(
            outgoing.at[step], out_ref.at[slot], rep_send.at[step], rep_recv.at[slot],
            device_id=(dp, peer), device_id_type=MESH,
        )

    cols = wk_ref.shape[1]

    def weight(src, dst, send, recv, peer, slot):
        return pltpu.make_async_remote_copy(
            src, dst.at[:, pl.ds(slot * cols, cols)], send.at[peer], recv.at[slot],
            device_id=(peer, me), device_id_type=MESH,
        )

    def weights(peer, slot):
        return (
            weight(wk_ref, wk_out, wk_send, wk_recv, peer, slot),
            weight(wv_ref, wv_out, wv_send, wv_recv, peer, slot),
        )

    own = (
        pltpu.make_async_copy(wk_ref, wk_out.at[:, pl.ds(dp * cols, cols)], own_sem.at[0]),
        pltpu.make_async_copy(wv_ref, wv_out.at[:, pl.ds(dp * cols, cols)], own_sem.at[1]),
    )

    barrier = pltpu.get_barrier_semaphore()

    def greet(k, carry):
        pl.semaphore_signal(barrier, inc=1, device_id=(dp, lax.rem(me + k, n)), device_id_type=MESH)
        return carry

    def greet_dp(k, carry):
        pl.semaphore_signal(barrier, inc=1, device_id=(lax.rem(dp + k, nd), me), device_id_type=MESH)
        return carry

    lax.fori_loop(1, n, greet, 0)
    lax.fori_loop(1, nd, greet_dp, 0)
    pl.semaphore_wait(barrier, n - 1 + nd - 1)

    def ask(k, carry):
        request(peer_of(k, 1), me).start()
        return carry

    lax.fori_loop(1, n, ask, 0)

    def share(k, carry):
        for copy in weights(lax.rem(dp + k, nd), dp):
            copy.start()
        return carry

    lax.fori_loop(1, nd, share, 0)
    for copy in own:
        copy.start()
    asked[me] = wanted_ref[me]

    def serve(c, carry):
        ids_list = []
        for j in range(group):
            k = c * group + j
            source = peer_of(k, -1)

            @pl.when(k > 0)
            def _():
                request(source, source).wait_recv()

            ids_list.append(asked[source])
        rows = gathered_rows(ids_list, table_ref, length)
        outgoing[pl.ds(c * group, group)] = rows.reshape(group, 2 * length, rows.shape[-1])
        for j in range(group):
            k = c * group + j
            source = peer_of(k, -1)

            @pl.when(k == 0)
            def _():
                out_ref[me] = outgoing[k]

            @pl.when(k > 0)
            def _():
                reply(k, source, me).start()

        return carry

    lax.fori_loop(0, n // group, serve, 0)

    def finish(k, carry):
        peer = peer_of(k, 1)
        request(peer, me).wait_send()
        reply(k, peer_of(k, -1), me).wait_send()
        reply(k, peer, peer).wait_recv()
        return carry

    lax.fori_loop(1, n, finish, 0)

    def gathered(k, carry):
        peer = lax.rem(dp + k, nd)
        for copy in weights(peer, dp):
            copy.wait_send()
        for copy in weights(peer, peer):
            copy.wait_recv()
        return carry

    lax.fori_loop(1, nd, gathered, 0)
    for copy in own:
        copy.wait()


def fetch(wanted, table, key_weight, value_weight, length, nd):
    n = wanted.shape[0]
    width = table.shape[1]
    vmem = pl.BlockSpec(memory_space=pltpu.VMEM)
    anywhere = pl.BlockSpec(memory_space=pl.ANY)
    return pl.pallas_call(
        functools.partial(fetch_kernel, length, math.gcd(8, n)),
        out_shape=(
            jax.ShapeDtypeStruct((n, 2 * length, width), table.dtype),
            jax.ShapeDtypeStruct((key_weight.shape[0], nd * key_weight.shape[1]), key_weight.dtype),
            jax.ShapeDtypeStruct((value_weight.shape[0], nd * value_weight.shape[1]), value_weight.dtype),
        ),
        in_specs=[vmem, vmem, anywhere, anywhere],
        out_specs=(vmem, anywhere, anywhere),
        scratch_shapes=[
            pltpu.VMEM(wanted.shape, jnp.int32),
            pltpu.VMEM((n, 2 * length, width), table.dtype),
            pltpu.SemaphoreType.DMA((n,)),
            pltpu.SemaphoreType.DMA((n,)),
            pltpu.SemaphoreType.DMA((n,)),
            pltpu.SemaphoreType.DMA((n,)),
            pltpu.SemaphoreType.DMA((nd,)),
            pltpu.SemaphoreType.DMA((nd,)),
            pltpu.SemaphoreType.DMA((nd,)),
            pltpu.SemaphoreType.DMA((nd,)),
            pltpu.SemaphoreType.DMA((2,)),
        ],
        compiler_params=pltpu.CompilerParams(collective_id=0, has_side_effects=True),
    )(wanted, table, key_weight, value_weight)


def normalize(nbr_rows, enc_gain):
    widened = nbr_rows.astype(jnp.float32)
    mean_square = jnp.mean(widened * widened, axis=-1, keepdims=True)
    return (widened * lax.rsqrt(mean_square + eps_norm) * enc_gain).astype(jnp.bfloat16)


def project(nbr_rows, enc_gain, key_weight, value_weight):
    group_count = nbr_rows.shape[0]
    normed = normalize(nbr_rows, enc_gain)
    flat_rows = normed.reshape(-1, normed.shape[-1])
    key_part = jnp.dot(flat_rows, key_weight, preferred_element_type=jnp.float32)
    value_part = jnp.dot(flat_rows, value_weight, preferred_element_type=jnp.float32)
    keys_out = key_part.astype(jnp.bfloat16)
    values_out = value_part.astype(jnp.bfloat16)
    return (
        keys_out.reshape(group_count, -1, keys_out.shape[-1]),
        values_out.reshape(group_count, -1, values_out.shape[-1]),
    )


def attend(grouped, keys_in, values_in):
    group_count = grouped.shape[0]
    query_heads = grouped.reshape(group_count, SPAN, HEADS, DH)
    key_heads = keys_in.reshape(group_count, -1, HEADS, DH)
    value_heads = values_in.reshape(group_count, -1, HEADS, DH)
    scores = jnp.einsum(
        "gqhd,gkhd->ghqk", query_heads, key_heads, preferred_element_type=jnp.float32
    ) * (1.0 / math.sqrt(DH))
    row_max = jnp.max(scores, axis=-1, keepdims=True)
    expo = jnp.exp(scores - row_max)
    probs_low = (expo / jnp.sum(expo, axis=-1, keepdims=True)).astype(jnp.bfloat16)
    mixed = jnp.einsum(
        "ghqk,gkhd->gqhd", probs_low, value_heads, preferred_element_type=jnp.float32
    )
    return mixed.reshape(group_count * SPAN, HEADS * DH).astype(jnp.bfloat16)


def body(queries, database, enc_gain, key_weight, value_weight, ret_shard, ret_row):
    spans = ret_shard.shape[0]
    nbr_count = ret_shard.shape[1]
    owners = lax.axis_size("seq")
    capacity = max(2, min(spans, 2 * spans * nbr_count // owners))
    requests = spans * nbr_count
    length = database.shape[1]
    enc_width = database.shape[2]
    shard_flat = ret_shard.reshape(requests)
    row_flat = ret_row.reshape(requests)
    order = jnp.arange(requests, dtype=jnp.int32)
    same_owner = shard_flat[:, None] == shard_flat[None, :]
    earlier = order[None, :] < order[:, None]
    slot_rank = jnp.sum(jnp.logical_and(same_owner, earlier), axis=1)
    owner_ids = jnp.arange(owners, dtype=jnp.int32)
    slot_ids = jnp.arange(capacity, dtype=jnp.int32)
    matches = jnp.logical_and(
        shard_flat[None, None, :] == owner_ids[:, None, None],
        slot_rank[None, None, :] == slot_ids[None, :, None],
    )
    wanted = jnp.sum(jnp.where(matches, row_flat[None, None, :] + 1, 0), axis=2) - 1
    wanted = jnp.broadcast_to(wanted[:, :, None], (owners, capacity, 128))
    wanted = jnp.pad(wanted, ((0, 0), (0, 8 - capacity), (0, 0)), constant_values=-1)
    table = database.reshape(database.shape[0] * length, enc_width)
    arrived, key_weight, value_weight = fetch(
        wanted, table, key_weight, value_weight, length, lax.axis_size("dp")
    )
    arrived = arrived.reshape(owners * capacity, length, enc_width)
    fetched = jnp.take(arrived, shard_flat * capacity + slot_rank, axis=0).reshape(
        spans, nbr_count, length, enc_width
    )
    prior_rows = from_behind(fetched[-1:], ("dp", "seq"), 1)
    keys_own, values_own = project(fetched, enc_gain, key_weight, value_weight)
    keys_prior, values_prior = project(prior_rows, enc_gain, key_weight, value_weight)
    keys_all = jnp.concatenate([keys_prior, keys_own], axis=0)
    values_all = jnp.concatenate([values_prior, values_own], axis=0)
    token_count = queries.shape[0]
    columns = queries.shape[1]
    padded = jnp.concatenate(
        [
            jnp.zeros((1, columns), queries.dtype),
            queries,
            jnp.zeros((SPAN - 1, columns), queries.dtype),
        ],
        axis=0,
    )
    grouped = padded.reshape(spans + 1, SPAN, columns)
    return attend(grouped, keys_all, values_all)[1 : 1 + token_count]


def solution(mesh):
    return jax.shard_map(
        body,
        mesh=mesh,
        in_specs=(
            P(("dp", "seq"), None),
            P("seq", None, None),
            P(),
            P(None, "dp"),
            P(None, "dp"),
            P(("dp", "seq"), None),
            P(("dp", "seq"), None),
        ),
        out_specs=P(("dp", "seq"), None),
        check_vma=False,
    )
```

```python
import functools
import math

import jax
import jax.numpy as jnp
from jax import lax
from jax.experimental import pallas as pl
from jax.experimental.pallas import tpu as pltpu
from jax.sharding import PartitionSpec as P

MESH = pl.DeviceIdType.MESH

HEADS = 16
DH = 128
SPAN = 64


eps_norm = 1e-06


def from_behind(block, axis, distance):
    devices = range(lax.axis_size(axis))
    route = [(i - distance, i) for i in devices if i - distance in devices]
    return lax.ppermute(block, axis, route)


def gathered_rows(ids_list, table_ref, length):
    pieces = []
    for ids in ids_list:
        for slot in range(2):
            pieces.append(jnp.broadcast_to(ids[slot : slot + 1, :], (length, 128)))
    sel = jnp.concatenate(pieces, axis=0)
    shape = sel.shape
    sub = lax.broadcasted_iota(jnp.int32, shape, 0)
    lane = lax.broadcasted_iota(jnp.int32, shape, 1)
    total = jnp.zeros((shape[0], table_ref.shape[1]), jnp.float32)
    for h in range(table_ref.shape[0] // 128):
        col = lane + h * 128
        hit = jnp.logical_and(col // length == sel, col % length == sub % length)
        total += jnp.dot(
            hit.astype(table_ref.dtype),
            table_ref[h * 128 : (h + 1) * 128, :],
            preferred_element_type=jnp.float32,
        )
    return total.astype(table_ref.dtype)


def torus_step(k, across, sign):
    i = k // across
    j = lax.rem(k, across)
    dz = sign * ((i + 1) // 2) * (2 * lax.rem(i, 2) - 1)
    dy = sign * ((j + 1) // 2) * (2 * lax.rem(j, 2) - 1)
    return dy, dz


def fetch_kernel(
    length, group, wanted_ref, table_ref, wk_ref, wv_ref, out_ref, wk_out, wv_out,
    asked, outgoing, req_send, req_recv, rep_send, rep_recv, wk_send, wk_recv, wv_send, wv_recv, own_sem,
):
    n = wanted_ref.shape[0]
    nd = wk_out.shape[1] // wk_ref.shape[1]
    me = lax.axis_index("seq")
    dp = lax.axis_index("dp")
    across = math.gcd(4, n)
    depth = n // across

    def peer_of(k, sign):
        dy, dz = torus_step(k, across, sign)
        y = lax.rem(me, across)
        z = me // across
        return lax.rem(z + dz + depth, depth) * across + lax.rem(y + dy + across, across)

    def request(peer, slot):
        return pltpu.make_async_remote_copy(
            wanted_ref.at[peer], asked.at[slot], req_send.at[peer], req_recv.at[slot],
            device_id=(dp, peer), device_id_type=MESH,
        )

    def reply(step, peer, slot):
        return pltpu.make_async_remote_copy(
            outgoing.at[step], out_ref.at[slot], rep_send.at[step], rep_recv.at[slot],
            device_id=(dp, peer), device_id_type=MESH,
        )

    cols = wk_ref.shape[1]

    def weight(src, dst, send, recv, peer, slot):
        return pltpu.make_async_remote_copy(
            src, dst.at[:, pl.ds(slot * cols, cols)], send.at[peer], recv.at[slot],
            device_id=(peer, me), device_id_type=MESH,
        )

    def weights(peer, slot):
        return (
            weight(wk_ref, wk_out, wk_send, wk_recv, peer, slot),
            weight(wv_ref, wv_out, wv_send, wv_recv, peer, slot),
        )

    own = (
        pltpu.make_async_copy(wk_ref, wk_out.at[:, pl.ds(dp * cols, cols)], own_sem.at[0]),
        pltpu.make_async_copy(wv_ref, wv_out.at[:, pl.ds(dp * cols, cols)], own_sem.at[1]),
    )

    barrier = pltpu.get_barrier_semaphore()

    def greet(k, carry):
        pl.semaphore_signal(barrier, inc=1, device_id=(dp, lax.rem(me + k, n)), device_id_type=MESH)
        return carry

    def greet_dp(k, carry):
        pl.semaphore_signal(barrier, inc=1, device_id=(lax.rem(dp + k, nd), me), device_id_type=MESH)
        return carry

    lax.fori_loop(1, n, greet, 0)
    lax.fori_loop(1, nd, greet_dp, 0)
    pl.semaphore_wait(barrier, n - 1 + nd - 1)

    def ask(k, carry):
        request(peer_of(k, 1), me).start()
        return carry

    lax.fori_loop(1, n, ask, 0)

    def share(k, carry):
        for copy in weights(lax.rem(dp + k, nd), dp):
            copy.start()
        return carry

    lax.fori_loop(1, nd, share, 0)
    for copy in own:
        copy.start()
    asked[me] = wanted_ref[me]

    def serve(c, carry):
        ids_list = []
        for j in range(group):
            k = c * group + j
            source = peer_of(k, -1)

            @pl.when(k > 0)
            def _():
                request(source, source).wait_recv()

            ids_list.append(asked[source])
        rows = gathered_rows(ids_list, table_ref, length)
        outgoing[pl.ds(c * group, group)] = rows.reshape(group, 2 * length, rows.shape[-1])
        for j in range(group):
            k = c * group + j
            source = peer_of(k, -1)

            @pl.when(k == 0)
            def _():
                out_ref[me] = outgoing[k]

            @pl.when(k > 0)
            def _():
                reply(k, source, me).start()

        return carry

    lax.fori_loop(0, n // group, serve, 0)

    def finish(k, carry):
        peer = peer_of(k, 1)
        request(peer, me).wait_send()
        reply(k, peer_of(k, -1), me).wait_send()
        reply(k, peer, peer).wait_recv()
        return carry

    lax.fori_loop(1, n, finish, 0)

    def gathered(k, carry):
        peer = lax.rem(dp + k, nd)
        for copy in weights(peer, dp):
            copy.wait_send()
        for copy in weights(peer, peer):
            copy.wait_recv()
        return carry

    lax.fori_loop(1, nd, gathered, 0)
    for copy in own:
        copy.wait()


def fetch(wanted, table, key_weight, value_weight, length, nd):
    n = wanted.shape[0]
    width = table.shape[1]
    vmem = pl.BlockSpec(memory_space=pltpu.VMEM)
    anywhere = pl.BlockSpec(memory_space=pl.ANY)
    return pl.pallas_call(
        functools.partial(fetch_kernel, length, math.gcd(8, n)),
        out_shape=(
            jax.ShapeDtypeStruct((n, 2 * length, width), table.dtype),
            jax.ShapeDtypeStruct((key_weight.shape[0], nd * key_weight.shape[1]), key_weight.dtype),
            jax.ShapeDtypeStruct((value_weight.shape[0], nd * value_weight.shape[1]), value_weight.dtype),
        ),
        in_specs=[vmem, vmem, anywhere, anywhere],
        out_specs=(vmem, anywhere, anywhere),
        scratch_shapes=[
            pltpu.VMEM(wanted.shape, jnp.int32),
            pltpu.VMEM((n, 2 * length, width), table.dtype),
            pltpu.SemaphoreType.DMA((n,)),
            pltpu.SemaphoreType.DMA((n,)),
            pltpu.SemaphoreType.DMA((n,)),
            pltpu.SemaphoreType.DMA((n,)),
            pltpu.SemaphoreType.DMA((nd,)),
            pltpu.SemaphoreType.DMA((nd,)),
            pltpu.SemaphoreType.DMA((nd,)),
            pltpu.SemaphoreType.DMA((nd,)),
            pltpu.SemaphoreType.DMA((2,)),
        ],
        compiler_params=pltpu.CompilerParams(collective_id=0, has_side_effects=True),
    )(wanted, table, key_weight, value_weight)


def normalize(nbr_rows, enc_gain):
    widened = nbr_rows.astype(jnp.float32)
    mean_square = jnp.mean(widened * widened, axis=-1, keepdims=True)
    return (widened * lax.rsqrt(mean_square + eps_norm) * enc_gain).astype(jnp.bfloat16)


def project(nbr_rows, enc_gain, key_weight, value_weight):
    group_count = nbr_rows.shape[0]
    normed = normalize(nbr_rows, enc_gain)
    flat_rows = normed.reshape(-1, normed.shape[-1])
    key_part = jnp.dot(flat_rows, key_weight, preferred_element_type=jnp.float32)
    value_part = jnp.dot(flat_rows, value_weight, preferred_element_type=jnp.float32)
    keys_out = key_part.astype(jnp.bfloat16)
    values_out = value_part.astype(jnp.bfloat16)
    return (
        keys_out.reshape(group_count, -1, keys_out.shape[-1]),
        values_out.reshape(group_count, -1, values_out.shape[-1]),
    )


def attend(grouped, keys_in, values_in):
    group_count = grouped.shape[0]
    query_heads = grouped.reshape(group_count, SPAN, HEADS, DH)
    key_heads = keys_in.reshape(group_count, -1, HEADS, DH)
    value_heads = values_in.reshape(group_count, -1, HEADS, DH)
    scores = jnp.einsum(
        "gqhd,gkhd->ghqk", query_heads, key_heads, preferred_element_type=jnp.float32
    ) * (1.0 / math.sqrt(DH))
    row_max = jnp.max(scores, axis=-1, keepdims=True)
    expo = jnp.exp(scores - row_max)
    probs_low = (expo / jnp.sum(expo, axis=-1, keepdims=True)).astype(jnp.bfloat16)
    mixed = jnp.einsum(
        "ghqk,gkhd->gqhd", probs_low, value_heads, preferred_element_type=jnp.float32
    )
    return mixed.reshape(group_count * SPAN, HEADS * DH).astype(jnp.bfloat16)


def body(queries, database, enc_gain, key_weight, value_weight, ret_shard, ret_row):
    spans = ret_shard.shape[0]
    nbr_count = ret_shard.shape[1]
    owners = lax.axis_size("seq")
    capacity = max(2, min(spans, 2 * spans * nbr_count // owners))
    requests = spans * nbr_count
    length = database.shape[1]
    enc_width = database.shape[2]
    shard_flat = ret_shard.reshape(requests)
    row_flat = ret_row.reshape(requests)
    order = jnp.arange(requests, dtype=jnp.int32)
    same_owner = shard_flat[:, None] == shard_flat[None, :]
    earlier = order[None, :] < order[:, None]
    slot_rank = jnp.sum(jnp.logical_and(same_owner, earlier), axis=1)
    owner_ids = jnp.arange(owners, dtype=jnp.int32)
    slot_ids = jnp.arange(capacity, dtype=jnp.int32)
    matches = jnp.logical_and(
        shard_flat[None, None, :] == owner_ids[:, None, None],
        slot_rank[None, None, :] == slot_ids[None, :, None],
    )
    wanted = jnp.sum(jnp.where(matches, row_flat[None, None, :] + 1, 0), axis=2) - 1
    wanted = jnp.broadcast_to(wanted[:, :, None], (owners, capacity, 128))
    wanted = jnp.pad(wanted, ((0, 0), (0, 8 - capacity), (0, 0)), constant_values=-1)
    table = database.reshape(database.shape[0] * length, enc_width)
    arrived, key_weight, value_weight = fetch(
        wanted, table, key_weight, value_weight, length, lax.axis_size("dp")
    )
    arrived = arrived.reshape(owners * capacity, length, enc_width)
    fetched = jnp.take(arrived, shard_flat * capacity + slot_rank, axis=0).reshape(
        spans, nbr_count, length, enc_width
    )
    token_count = queries.shape[0]
    columns = queries.shape[1]
    padded = jnp.concatenate(
        [
            jnp.zeros((1, columns), queries.dtype),
            queries,
            jnp.zeros((SPAN - 1, columns), queries.dtype),
        ],
        axis=0,
    )
    grouped = padded.reshape(spans + 1, SPAN, columns)
    keys_own, values_own = project(fetched, enc_gain, key_weight, value_weight)
    own_out = attend(grouped[1:], keys_own, values_own)
    last_rows, own_out = lax.optimization_barrier((fetched[-1:], own_out))
    prior_rows = from_behind(last_rows, ("dp", "seq"), 1)
    keys_prior, values_prior = project(prior_rows, enc_gain, key_weight, value_weight)
    prior_out = attend(grouped[:1], keys_prior, values_prior)
    return jnp.concatenate([prior_out[1:], own_out[: token_count - SPAN + 1]], axis=0)

def solution(mesh):
    return jax.shard_map(
        body,
        mesh=mesh,
        in_specs=(
            P(("dp", "seq"), None),
            P("seq", None, None),
            P(),
            P(None, "dp"),
            P(None, "dp"),
            P(("dp", "seq"), None),
            P(("dp", "seq"), None),
        ),
        out_specs=P(("dp", "seq"), None),
        check_vma=False,
    )
```

```python
import functools
import math

import jax
import jax.numpy as jnp
from jax import lax
from jax.experimental import pallas as pl
from jax.experimental.pallas import tpu as pltpu
from jax.sharding import PartitionSpec as P

MESH = pl.DeviceIdType.MESH

HEADS = 16
DH = 128
SPAN = 64


eps_norm = 1e-06


def from_behind(block, axis, distance):
    devices = range(lax.axis_size(axis))
    route = [(i - distance, i) for i in devices if i - distance in devices]
    return lax.ppermute(block, axis, route)


def gathered_rows(ids_list, table_ref, length):
    pieces = []
    for ids in ids_list:
        for slot in range(2):
            pieces.append(jnp.broadcast_to(ids[slot : slot + 1, :], (length, 128)))
    sel = jnp.concatenate(pieces, axis=0)
    shape = sel.shape
    sub = lax.broadcasted_iota(jnp.int32, shape, 0)
    lane = lax.broadcasted_iota(jnp.int32, shape, 1)
    total = jnp.zeros((shape[0], table_ref.shape[1]), jnp.float32)
    for h in range(table_ref.shape[0] // 128):
        col = lane + h * 128
        hit = jnp.logical_and(col // length == sel, col % length == sub % length)
        total += jnp.dot(
            hit.astype(table_ref.dtype),
            table_ref[h * 128 : (h + 1) * 128, :],
            preferred_element_type=jnp.float32,
        )
    return total.astype(table_ref.dtype)


def torus_step(k, across, depth, sign):
    i = lax.rem(depth - k // across, depth)
    j = lax.rem(k, across)
    dz = sign * ((i + 1) // 2) * (2 * lax.rem(i, 2) - 1)
    dy = sign * ((j + 1) // 2) * (2 * lax.rem(j, 2) - 1)
    return dy, dz


def fetch_kernel(
    length, group, wanted_ref, table_ref, wk_ref, wv_ref, out_ref, wk_out, wv_out,
    asked, outgoing, req_send, req_recv, rep_send, rep_recv, wk_send, wk_recv, wv_send, wv_recv, own_sem,
):
    n = wanted_ref.shape[0]
    nd = wk_out.shape[1] // wk_ref.shape[1]
    me = lax.axis_index("seq")
    dp = lax.axis_index("dp")
    across = math.gcd(4, n)
    depth = n // across

    def peer_of(k, sign):
        dy, dz = torus_step(k, across, depth, sign)
        y = lax.rem(me, across)
        z = me // across
        return lax.rem(z + dz + depth, depth) * across + lax.rem(y + dy + across, across)

    def request(peer, slot):
        return pltpu.make_async_remote_copy(
            wanted_ref.at[peer], asked.at[slot], req_send.at[peer], req_recv.at[slot],
            device_id=(dp, peer), device_id_type=MESH,
        )

    def reply(step, peer, slot):
        return pltpu.make_async_remote_copy(
            outgoing.at[step], out_ref.at[slot], rep_send.at[step], rep_recv.at[slot],
            device_id=(dp, peer), device_id_type=MESH,
        )

    cols = wk_ref.shape[1]

    def weight(src, dst, send, recv, peer, slot):
        return pltpu.make_async_remote_copy(
            src, dst.at[:, pl.ds(slot * cols, cols)], send.at[peer], recv.at[slot],
            device_id=(peer, me), device_id_type=MESH,
        )

    def weights(peer, slot):
        return (
            weight(wk_ref, wk_out, wk_send, wk_recv, peer, slot),
            weight(wv_ref, wv_out, wv_send, wv_recv, peer, slot),
        )

    own = (
        pltpu.make_async_copy(wk_ref, wk_out.at[:, pl.ds(dp * cols, cols)], own_sem.at[0]),
        pltpu.make_async_copy(wv_ref, wv_out.at[:, pl.ds(dp * cols, cols)], own_sem.at[1]),
    )

    barrier = pltpu.get_barrier_semaphore()

    def greet(k, carry):
        pl.semaphore_signal(barrier, inc=1, device_id=(dp, lax.rem(me + k, n)), device_id_type=MESH)
        return carry

    def greet_dp(k, carry):
        pl.semaphore_signal(barrier, inc=1, device_id=(lax.rem(dp + k, nd), me), device_id_type=MESH)
        return carry

    lax.fori_loop(1, n, greet, 0)
    lax.fori_loop(1, nd, greet_dp, 0)
    pl.semaphore_wait(barrier, n - 1 + nd - 1)

    def ask(k, carry):
        request(peer_of(k, 1), me).start()
        return carry

    lax.fori_loop(1, n, ask, 0)

    def share(k, carry):
        for copy in weights(lax.rem(dp + k, nd), dp):
            copy.start()
        return carry

    lax.fori_loop(1, nd, share, 0)
    for copy in own:
        copy.start()
    asked[me] = wanted_ref[me]

    def serve(c, carry):
        ids_list = []
        for j in range(group):
            k = c * group + j
            source = peer_of(k, -1)

            @pl.when(k > 0)
            def _():
                request(source, source).wait_recv()

            ids_list.append(asked[source])
        rows = gathered_rows(ids_list, table_ref, length)
        outgoing[pl.ds(c * group, group)] = rows.reshape(group, 2 * length, rows.shape[-1])
        for j in range(group):
            k = c * group + j
            source = peer_of(k, -1)

            @pl.when(k == 0)
            def _():
                out_ref[me] = outgoing[k]

            @pl.when(k > 0)
            def _():
                reply(k, source, me).start()

        return carry

    lax.fori_loop(0, n // group, serve, 0)

    def finish(k, carry):
        peer = peer_of(k, 1)
        request(peer, me).wait_send()
        reply(k, peer_of(k, -1), me).wait_send()
        reply(k, peer, peer).wait_recv()
        return carry

    lax.fori_loop(1, n, finish, 0)

    def gathered(k, carry):
        peer = lax.rem(dp + k, nd)
        for copy in weights(peer, dp):
            copy.wait_send()
        for copy in weights(peer, peer):
            copy.wait_recv()
        return carry

    lax.fori_loop(1, nd, gathered, 0)
    for copy in own:
        copy.wait()


def fetch(wanted, table, key_weight, value_weight, length, nd):
    n = wanted.shape[0]
    width = table.shape[1]
    vmem = pl.BlockSpec(memory_space=pltpu.VMEM)
    anywhere = pl.BlockSpec(memory_space=pl.ANY)
    return pl.pallas_call(
        functools.partial(fetch_kernel, length, math.gcd(8, n)),
        out_shape=(
            jax.ShapeDtypeStruct((n, 2 * length, width), table.dtype),
            jax.ShapeDtypeStruct((key_weight.shape[0], nd * key_weight.shape[1]), key_weight.dtype),
            jax.ShapeDtypeStruct((value_weight.shape[0], nd * value_weight.shape[1]), value_weight.dtype),
        ),
        in_specs=[vmem, vmem, anywhere, anywhere],
        out_specs=(vmem, anywhere, anywhere),
        scratch_shapes=[
            pltpu.VMEM(wanted.shape, jnp.int32),
            pltpu.VMEM((n, 2 * length, width), table.dtype),
            pltpu.SemaphoreType.DMA((n,)),
            pltpu.SemaphoreType.DMA((n,)),
            pltpu.SemaphoreType.DMA((n,)),
            pltpu.SemaphoreType.DMA((n,)),
            pltpu.SemaphoreType.DMA((nd,)),
            pltpu.SemaphoreType.DMA((nd,)),
            pltpu.SemaphoreType.DMA((nd,)),
            pltpu.SemaphoreType.DMA((nd,)),
            pltpu.SemaphoreType.DMA((2,)),
        ],
        compiler_params=pltpu.CompilerParams(collective_id=0, has_side_effects=True),
    )(wanted, table, key_weight, value_weight)


def normalize(nbr_rows, enc_gain):
    widened = nbr_rows.astype(jnp.float32)
    mean_square = jnp.mean(widened * widened, axis=-1, keepdims=True)
    return (widened * lax.rsqrt(mean_square + eps_norm) * enc_gain).astype(jnp.bfloat16)


def project(nbr_rows, enc_gain, key_weight, value_weight):
    group_count = nbr_rows.shape[0]
    normed = normalize(nbr_rows, enc_gain)
    flat_rows = normed.reshape(-1, normed.shape[-1])
    key_part = jnp.dot(flat_rows, key_weight, preferred_element_type=jnp.float32)
    value_part = jnp.dot(flat_rows, value_weight, preferred_element_type=jnp.float32)
    keys_out = key_part.astype(jnp.bfloat16)
    values_out = value_part.astype(jnp.bfloat16)
    return (
        keys_out.reshape(group_count, -1, keys_out.shape[-1]),
        values_out.reshape(group_count, -1, values_out.shape[-1]),
    )


def attend(grouped, keys_in, values_in):
    group_count = grouped.shape[0]
    query_heads = grouped.reshape(group_count, SPAN, HEADS, DH)
    key_heads = keys_in.reshape(group_count, -1, HEADS, DH)
    value_heads = values_in.reshape(group_count, -1, HEADS, DH)
    scores = jnp.einsum(
        "gqhd,gkhd->ghqk", query_heads, key_heads, preferred_element_type=jnp.float32
    ) * (1.0 / math.sqrt(DH))
    row_max = jnp.max(scores, axis=-1, keepdims=True)
    expo = jnp.exp(scores - row_max)
    probs_low = (expo / jnp.sum(expo, axis=-1, keepdims=True)).astype(jnp.bfloat16)
    mixed = jnp.einsum(
        "ghqk,gkhd->gqhd", probs_low, value_heads, preferred_element_type=jnp.float32
    )
    return mixed.reshape(group_count * SPAN, HEADS * DH).astype(jnp.bfloat16)


def body(queries, database, enc_gain, key_weight, value_weight, ret_shard, ret_row):
    spans = ret_shard.shape[0]
    nbr_count = ret_shard.shape[1]
    owners = lax.axis_size("seq")
    capacity = max(2, min(spans, 2 * spans * nbr_count // owners))
    requests = spans * nbr_count
    length = database.shape[1]
    enc_width = database.shape[2]
    shard_flat = ret_shard.reshape(requests)
    row_flat = ret_row.reshape(requests)
    order = jnp.arange(requests, dtype=jnp.int32)
    same_owner = shard_flat[:, None] == shard_flat[None, :]
    earlier = order[None, :] < order[:, None]
    slot_rank = jnp.sum(jnp.logical_and(same_owner, earlier), axis=1)
    owner_ids = jnp.arange(owners, dtype=jnp.int32)
    slot_ids = jnp.arange(capacity, dtype=jnp.int32)
    matches = jnp.logical_and(
        shard_flat[None, None, :] == owner_ids[:, None, None],
        slot_rank[None, None, :] == slot_ids[None, :, None],
    )
    wanted = jnp.sum(jnp.where(matches, row_flat[None, None, :] + 1, 0), axis=2) - 1
    wanted = jnp.broadcast_to(wanted[:, :, None], (owners, capacity, 128))
    wanted = jnp.pad(wanted, ((0, 0), (0, 8 - capacity), (0, 0)), constant_values=-1)
    table = database.reshape(database.shape[0] * length, enc_width)
    arrived, key_weight, value_weight = fetch(
        wanted, table, key_weight, value_weight, length, lax.axis_size("dp")
    )
    arrived = arrived.reshape(owners * capacity, length, enc_width)
    fetched = jnp.take(arrived, shard_flat * capacity + slot_rank, axis=0).reshape(
        spans, nbr_count, length, enc_width
    )
    prior_rows = from_behind(fetched[-1:], ("dp", "seq"), 1)
    keys_own, values_own = project(fetched, enc_gain, key_weight, value_weight)
    keys_prior, values_prior = project(prior_rows, enc_gain, key_weight, value_weight)
    keys_all = jnp.concatenate([keys_prior, keys_own], axis=0)
    values_all = jnp.concatenate([values_prior, values_own], axis=0)
    token_count = queries.shape[0]
    columns = queries.shape[1]
    padded = jnp.concatenate(
        [
            jnp.zeros((1, columns), queries.dtype),
            queries,
            jnp.zeros((SPAN - 1, columns), queries.dtype),
        ],
        axis=0,
    )
    grouped = padded.reshape(spans + 1, SPAN, columns)
    return attend(grouped, keys_all, values_all)[1 : 1 + token_count]


def solution(mesh):
    return jax.shard_map(
        body,
        mesh=mesh,
        in_specs=(
            P(("dp", "seq"), None),
            P("seq", None, None),
            P(),
            P(None, "dp"),
            P(None, "dp"),
            P(("dp", "seq"), None),
            P(("dp", "seq"), None),
        ),
        out_specs=P(("dp", "seq"), None),
        check_vma=False,
    )
```

```python
import functools
import math

import jax
import jax.numpy as jnp
from jax import lax
from jax.experimental import pallas as pl
from jax.experimental.pallas import tpu as pltpu
from jax.sharding import PartitionSpec as P

MESH = pl.DeviceIdType.MESH

HEADS = 16
DH = 128
SPAN = 64


eps_norm = 1e-06


def from_behind(block, axis, distance):
    devices = range(lax.axis_size(axis))
    route = [(i - distance, i) for i in devices if i - distance in devices]
    return lax.ppermute(block, axis, route)


def gathered_rows(ids_list, table_ref, length):
    pieces = []
    for ids in ids_list:
        for slot in range(2):
            pieces.append(jnp.broadcast_to(ids[slot : slot + 1, :], (length, 128)))
    sel = jnp.concatenate(pieces, axis=0)
    shape = sel.shape
    sub = lax.broadcasted_iota(jnp.int32, shape, 0)
    lane = lax.broadcasted_iota(jnp.int32, shape, 1)
    total = jnp.zeros((shape[0], table_ref.shape[1]), jnp.float32)
    for h in range(table_ref.shape[0] // 128):
        col = lane + h * 128
        hit = jnp.logical_and(col // length == sel, col % length == sub % length)
        total += jnp.dot(
            hit.astype(table_ref.dtype),
            table_ref[h * 128 : (h + 1) * 128, :],
            preferred_element_type=jnp.float32,
        )
    return total.astype(table_ref.dtype)


def torus_step(k, across, depth, sign):
    i = lax.rem(depth - k // across, depth)
    j = lax.rem(k, across)
    dz = sign * ((i + 1) // 2) * (2 * lax.rem(i, 2) - 1)
    dy = sign * ((j + 1) // 2) * (2 * lax.rem(j, 2) - 1)
    return dy, dz


def fetch_kernel(
    length, group, wanted_ref, table_ref, wk_ref, wv_ref, out_ref, wk_out, wv_out,
    asked, outgoing, req_send, req_recv, rep_send, rep_recv, wk_send, wk_recv, wv_send, wv_recv, own_sem,
):
    n = wanted_ref.shape[0]
    nd = wk_out.shape[1] // wk_ref.shape[1]
    me = lax.axis_index("seq")
    dp = lax.axis_index("dp")
    across = math.gcd(4, n)
    depth = n // across

    def peer_of(k, sign):
        dy, dz = torus_step(k, across, depth, sign)
        y = lax.rem(me, across)
        z = me // across
        return lax.rem(z + dz + depth, depth) * across + lax.rem(y + dy + across, across)

    def request(peer, slot):
        return pltpu.make_async_remote_copy(
            wanted_ref.at[peer], asked.at[slot], req_send.at[peer], req_recv.at[slot],
            device_id=(dp, peer), device_id_type=MESH,
        )

    def reply(step, peer, slot):
        return pltpu.make_async_remote_copy(
            outgoing.at[step], out_ref.at[slot], rep_send.at[step], rep_recv.at[slot],
            device_id=(dp, peer), device_id_type=MESH,
        )

    cols = wk_ref.shape[1]

    def weight(src, dst, send, recv, peer, slot):
        return pltpu.make_async_remote_copy(
            src, dst.at[:, pl.ds(slot * cols, cols)], send.at[peer], recv.at[slot],
            device_id=(peer, me), device_id_type=MESH,
        )

    def weights(peer, slot):
        return (
            weight(wk_ref, wk_out, wk_send, wk_recv, peer, slot),
            weight(wv_ref, wv_out, wv_send, wv_recv, peer, slot),
        )

    own = (
        pltpu.make_async_copy(wk_ref, wk_out.at[:, pl.ds(dp * cols, cols)], own_sem.at[0]),
        pltpu.make_async_copy(wv_ref, wv_out.at[:, pl.ds(dp * cols, cols)], own_sem.at[1]),
    )

    barrier = pltpu.get_barrier_semaphore()

    def greet(k, carry):
        pl.semaphore_signal(barrier, inc=1, device_id=(dp, lax.rem(me + k, n)), device_id_type=MESH)
        return carry

    def greet_dp(k, carry):
        pl.semaphore_signal(barrier, inc=1, device_id=(lax.rem(dp + k, nd), me), device_id_type=MESH)
        return carry

    lax.fori_loop(1, n, greet, 0)
    lax.fori_loop(1, nd, greet_dp, 0)
    pl.semaphore_wait(barrier, n - 1 + nd - 1)

    def ask(k, carry):
        request(peer_of(k, 1), me).start()
        return carry

    lax.fori_loop(1, n, ask, 0)

    def share(k, carry):
        for copy in weights(lax.rem(dp + k, nd), dp):
            copy.start()
        return carry

    asked[me] = wanted_ref[me]

    def serve(c, carry):
        ids_list = []
        for j in range(group):
            k = c * group + j
            source = peer_of(k, -1)

            @pl.when(k > 0)
            def _():
                request(source, source).wait_recv()

            ids_list.append(asked[source])
        rows = gathered_rows(ids_list, table_ref, length)
        outgoing[pl.ds(c * group, group)] = rows.reshape(group, 2 * length, rows.shape[-1])
        for j in range(group):
            k = c * group + j
            source = peer_of(k, -1)

            @pl.when(k == 0)
            def _():
                out_ref[me] = outgoing[k]

            @pl.when(k > 0)
            def _():
                reply(k, source, me).start()

        return carry

    lax.fori_loop(0, n // group, serve, 0)
    lax.fori_loop(1, nd, share, 0)
    for copy in own:
        copy.start()

    def finish(k, carry):
        peer = peer_of(k, 1)
        request(peer, me).wait_send()
        reply(k, peer_of(k, -1), me).wait_send()
        reply(k, peer, peer).wait_recv()
        return carry

    lax.fori_loop(1, n, finish, 0)

    def gathered(k, carry):
        peer = lax.rem(dp + k, nd)
        for copy in weights(peer, dp):
            copy.wait_send()
        for copy in weights(peer, peer):
            copy.wait_recv()
        return carry

    lax.fori_loop(1, nd, gathered, 0)
    for copy in own:
        copy.wait()


def fetch(wanted, table, key_weight, value_weight, length, nd):
    n = wanted.shape[0]
    width = table.shape[1]
    vmem = pl.BlockSpec(memory_space=pltpu.VMEM)
    anywhere = pl.BlockSpec(memory_space=pl.ANY)
    return pl.pallas_call(
        functools.partial(fetch_kernel, length, math.gcd(8, n)),
        out_shape=(
            jax.ShapeDtypeStruct((n, 2 * length, width), table.dtype),
            jax.ShapeDtypeStruct((key_weight.shape[0], nd * key_weight.shape[1]), key_weight.dtype),
            jax.ShapeDtypeStruct((value_weight.shape[0], nd * value_weight.shape[1]), value_weight.dtype),
        ),
        in_specs=[vmem, vmem, anywhere, anywhere],
        out_specs=(vmem, anywhere, anywhere),
        scratch_shapes=[
            pltpu.VMEM(wanted.shape, jnp.int32),
            pltpu.VMEM((n, 2 * length, width), table.dtype),
            pltpu.SemaphoreType.DMA((n,)),
            pltpu.SemaphoreType.DMA((n,)),
            pltpu.SemaphoreType.DMA((n,)),
            pltpu.SemaphoreType.DMA((n,)),
            pltpu.SemaphoreType.DMA((nd,)),
            pltpu.SemaphoreType.DMA((nd,)),
            pltpu.SemaphoreType.DMA((nd,)),
            pltpu.SemaphoreType.DMA((nd,)),
            pltpu.SemaphoreType.DMA((2,)),
        ],
        compiler_params=pltpu.CompilerParams(collective_id=0, has_side_effects=True),
    )(wanted, table, key_weight, value_weight)


def normalize(nbr_rows, enc_gain):
    widened = nbr_rows.astype(jnp.float32)
    mean_square = jnp.mean(widened * widened, axis=-1, keepdims=True)
    return (widened * lax.rsqrt(mean_square + eps_norm) * enc_gain).astype(jnp.bfloat16)


def project(nbr_rows, enc_gain, key_weight, value_weight):
    group_count = nbr_rows.shape[0]
    normed = normalize(nbr_rows, enc_gain)
    flat_rows = normed.reshape(-1, normed.shape[-1])
    key_part = jnp.dot(flat_rows, key_weight, preferred_element_type=jnp.float32)
    value_part = jnp.dot(flat_rows, value_weight, preferred_element_type=jnp.float32)
    keys_out = key_part.astype(jnp.bfloat16)
    values_out = value_part.astype(jnp.bfloat16)
    return (
        keys_out.reshape(group_count, -1, keys_out.shape[-1]),
        values_out.reshape(group_count, -1, values_out.shape[-1]),
    )


def attend(grouped, keys_in, values_in):
    group_count = grouped.shape[0]
    query_heads = grouped.reshape(group_count, SPAN, HEADS, DH)
    key_heads = keys_in.reshape(group_count, -1, HEADS, DH)
    value_heads = values_in.reshape(group_count, -1, HEADS, DH)
    scores = jnp.einsum(
        "gqhd,gkhd->ghqk", query_heads, key_heads, preferred_element_type=jnp.float32
    ) * (1.0 / math.sqrt(DH))
    row_max = jnp.max(scores, axis=-1, keepdims=True)
    expo = jnp.exp(scores - row_max)
    probs_low = (expo / jnp.sum(expo, axis=-1, keepdims=True)).astype(jnp.bfloat16)
    mixed = jnp.einsum(
        "ghqk,gkhd->gqhd", probs_low, value_heads, preferred_element_type=jnp.float32
    )
    return mixed.reshape(group_count * SPAN, HEADS * DH).astype(jnp.bfloat16)


def body(queries, database, enc_gain, key_weight, value_weight, ret_shard, ret_row):
    spans = ret_shard.shape[0]
    nbr_count = ret_shard.shape[1]
    owners = lax.axis_size("seq")
    capacity = max(2, min(spans, 2 * spans * nbr_count // owners))
    requests = spans * nbr_count
    length = database.shape[1]
    enc_width = database.shape[2]
    shard_flat = ret_shard.reshape(requests)
    row_flat = ret_row.reshape(requests)
    order = jnp.arange(requests, dtype=jnp.int32)
    same_owner = shard_flat[:, None] == shard_flat[None, :]
    earlier = order[None, :] < order[:, None]
    slot_rank = jnp.sum(jnp.logical_and(same_owner, earlier), axis=1)
    owner_ids = jnp.arange(owners, dtype=jnp.int32)
    slot_ids = jnp.arange(capacity, dtype=jnp.int32)
    matches = jnp.logical_and(
        shard_flat[None, None, :] == owner_ids[:, None, None],
        slot_rank[None, None, :] == slot_ids[None, :, None],
    )
    wanted = jnp.sum(jnp.where(matches, row_flat[None, None, :] + 1, 0), axis=2) - 1
    wanted = jnp.broadcast_to(wanted[:, :, None], (owners, capacity, 128))
    wanted = jnp.pad(wanted, ((0, 0), (0, 8 - capacity), (0, 0)), constant_values=-1)
    table = database.reshape(database.shape[0] * length, enc_width)
    arrived, key_weight, value_weight = fetch(
        wanted, table, key_weight, value_weight, length, lax.axis_size("dp")
    )
    arrived = arrived.reshape(owners * capacity, length, enc_width)
    fetched = jnp.take(arrived, shard_flat * capacity + slot_rank, axis=0).reshape(
        spans, nbr_count, length, enc_width
    )
    prior_rows = from_behind(fetched[-1:], ("dp", "seq"), 1)
    keys_own, values_own = project(fetched, enc_gain, key_weight, value_weight)
    keys_prior, values_prior = project(prior_rows, enc_gain, key_weight, value_weight)
    keys_all = jnp.concatenate([keys_prior, keys_own], axis=0)
    values_all = jnp.concatenate([values_prior, values_own], axis=0)
    token_count = queries.shape[0]
    columns = queries.shape[1]
    padded = jnp.concatenate(
        [
            jnp.zeros((1, columns), queries.dtype),
            queries,
            jnp.zeros((SPAN - 1, columns), queries.dtype),
        ],
        axis=0,
    )
    grouped = padded.reshape(spans + 1, SPAN, columns)
    return attend(grouped, keys_all, values_all)[1 : 1 + token_count]


def solution(mesh):
    return jax.shard_map(
        body,
        mesh=mesh,
        in_specs=(
            P(("dp", "seq"), None),
            P("seq", None, None),
            P(),
            P(None, "dp"),
            P(None, "dp"),
            P(("dp", "seq"), None),
            P(("dp", "seq"), None),
        ),
        out_specs=P(("dp", "seq"), None),
        check_vma=False,
    )
```

```python
import functools
import math

import jax
import jax.numpy as jnp
from jax import lax
from jax.experimental import pallas as pl
from jax.experimental.pallas import tpu as pltpu
from jax.sharding import PartitionSpec as P

MESH = pl.DeviceIdType.MESH

HEADS = 16
DH = 128
SPAN = 64


eps_norm = 1e-06


def from_behind(block, axis, distance):
    devices = range(lax.axis_size(axis))
    route = [(i - distance, i) for i in devices if i - distance in devices]
    return lax.ppermute(block, axis, route)


def gathered_rows(ids_list, table_ref, length):
    pieces = []
    for ids in ids_list:
        for slot in range(2):
            pieces.append(jnp.broadcast_to(ids[slot : slot + 1, :], (length, 128)))
    sel = jnp.concatenate(pieces, axis=0)
    shape = sel.shape
    sub = lax.broadcasted_iota(jnp.int32, shape, 0)
    lane = lax.broadcasted_iota(jnp.int32, shape, 1)
    total = jnp.zeros((shape[0], table_ref.shape[1]), jnp.float32)
    for h in range(table_ref.shape[0] // 128):
        col = lane + h * 128
        hit = jnp.logical_and(col // length == sel, col % length == sub % length)
        total += jnp.dot(
            hit.astype(table_ref.dtype),
            table_ref[h * 128 : (h + 1) * 128, :],
            preferred_element_type=jnp.float32,
        )
    return total.astype(table_ref.dtype)


def torus_step(k, across, depth, sign):
    i = lax.rem(depth - k // across, depth)
    j = lax.rem(k, across)
    dz = sign * ((i + 1) // 2) * (2 * lax.rem(i, 2) - 1)
    dy = sign * ((j + 1) // 2) * (2 * lax.rem(j, 2) - 1)
    return dy, dz


def fetch_kernel(
    length, group, wanted_ref, table_ref, wk_ref, wv_ref, out_ref, wk_out, wv_out,
    asked, outgoing, req_send, req_recv, rep_send, rep_recv, wk_send, wk_recv, wv_send, wv_recv, own_sem,
):
    n = wanted_ref.shape[0]
    nd = wk_out.shape[1] // wk_ref.shape[1]
    me = lax.axis_index("seq")
    dp = lax.axis_index("dp")
    across = math.gcd(4, n)
    depth = n // across

    def peer_of(k, sign):
        dy, dz = torus_step(k, across, depth, sign)
        y = lax.rem(me, across)
        z = me // across
        return lax.rem(z + dz + depth, depth) * across + lax.rem(y + dy + across, across)

    def request(peer, slot):
        return pltpu.make_async_remote_copy(
            wanted_ref.at[peer], asked.at[slot], req_send.at[peer], req_recv.at[slot],
            device_id=(dp, peer), device_id_type=MESH,
        )

    def reply(step, peer, slot):
        return pltpu.make_async_remote_copy(
            outgoing.at[step], out_ref.at[slot], rep_send.at[step], rep_recv.at[slot],
            device_id=(dp, peer), device_id_type=MESH,
        )

    cols = wk_ref.shape[1]

    def weight(src, dst, send, recv, peer, slot):
        return pltpu.make_async_remote_copy(
            src, dst.at[:, pl.ds(slot * cols, cols)], send.at[peer], recv.at[slot],
            device_id=(peer, me), device_id_type=MESH,
        )

    def weights(peer, slot):
        return (
            weight(wk_ref, wk_out, wk_send, wk_recv, peer, slot),
            weight(wv_ref, wv_out, wv_send, wv_recv, peer, slot),
        )

    own = (
        pltpu.make_async_copy(wk_ref, wk_out.at[:, pl.ds(dp * cols, cols)], own_sem.at[0]),
        pltpu.make_async_copy(wv_ref, wv_out.at[:, pl.ds(dp * cols, cols)], own_sem.at[1]),
    )

    barrier = pltpu.get_barrier_semaphore()

    def greet(k, carry):
        pl.semaphore_signal(barrier, inc=1, device_id=(dp, lax.rem(me + k, n)), device_id_type=MESH)
        return carry

    def greet_dp(k, carry):
        pl.semaphore_signal(barrier, inc=1, device_id=(lax.rem(dp + k, nd), me), device_id_type=MESH)
        return carry

    lax.fori_loop(1, n, greet, 0)
    lax.fori_loop(1, nd, greet_dp, 0)
    pl.semaphore_wait(barrier, n - 1 + nd - 1)

    def share(k, carry):
        for copy in weights(lax.rem(dp + k, nd), dp):
            copy.start()
        return carry

    lax.fori_loop(1, nd, share, 0)
    for copy in own:
        copy.start()

    def ask(k, carry):
        request(peer_of(k, 1), me).start()
        return carry

    lax.fori_loop(1, n, ask, 0)

    asked[me] = wanted_ref[me]

    def serve(c, carry):
        ids_list = []
        for j in range(group):
            k = c * group + j
            source = peer_of(k, -1)

            @pl.when(k > 0)
            def _():
                request(source, source).wait_recv()

            ids_list.append(asked[source])
        rows = gathered_rows(ids_list, table_ref, length)
        outgoing[pl.ds(c * group, group)] = rows.reshape(group, 2 * length, rows.shape[-1])
        for j in range(group):
            k = c * group + j
            source = peer_of(k, -1)

            @pl.when(k == 0)
            def _():
                out_ref[me] = outgoing[k]

            @pl.when(k > 0)
            def _():
                reply(k, source, me).start()

        return carry

    lax.fori_loop(0, n // group, serve, 0)

    def finish(k, carry):
        peer = peer_of(k, 1)
        request(peer, me).wait_send()
        reply(k, peer_of(k, -1), me).wait_send()
        reply(k, peer, peer).wait_recv()
        return carry

    lax.fori_loop(1, n, finish, 0)

    def gathered(k, carry):
        peer = lax.rem(dp + k, nd)
        for copy in weights(peer, dp):
            copy.wait_send()
        for copy in weights(peer, peer):
            copy.wait_recv()
        return carry

    lax.fori_loop(1, nd, gathered, 0)
    for copy in own:
        copy.wait()


def fetch(wanted, table, key_weight, value_weight, length, nd):
    n = wanted.shape[0]
    width = table.shape[1]
    vmem = pl.BlockSpec(memory_space=pltpu.VMEM)
    anywhere = pl.BlockSpec(memory_space=pl.ANY)
    return pl.pallas_call(
        functools.partial(fetch_kernel, length, math.gcd(8, n)),
        out_shape=(
            jax.ShapeDtypeStruct((n, 2 * length, width), table.dtype),
            jax.ShapeDtypeStruct((key_weight.shape[0], nd * key_weight.shape[1]), key_weight.dtype),
            jax.ShapeDtypeStruct((value_weight.shape[0], nd * value_weight.shape[1]), value_weight.dtype),
        ),
        in_specs=[vmem, vmem, anywhere, anywhere],
        out_specs=(vmem, anywhere, anywhere),
        scratch_shapes=[
            pltpu.VMEM(wanted.shape, jnp.int32),
            pltpu.VMEM((n, 2 * length, width), table.dtype),
            pltpu.SemaphoreType.DMA((n,)),
            pltpu.SemaphoreType.DMA((n,)),
            pltpu.SemaphoreType.DMA((n,)),
            pltpu.SemaphoreType.DMA((n,)),
            pltpu.SemaphoreType.DMA((nd,)),
            pltpu.SemaphoreType.DMA((nd,)),
            pltpu.SemaphoreType.DMA((nd,)),
            pltpu.SemaphoreType.DMA((nd,)),
            pltpu.SemaphoreType.DMA((2,)),
        ],
        compiler_params=pltpu.CompilerParams(collective_id=0, has_side_effects=True),
    )(wanted, table, key_weight, value_weight)


def normalize(nbr_rows, enc_gain):
    widened = nbr_rows.astype(jnp.float32)
    mean_square = jnp.mean(widened * widened, axis=-1, keepdims=True)
    return (widened * lax.rsqrt(mean_square + eps_norm) * enc_gain).astype(jnp.bfloat16)


def project(nbr_rows, enc_gain, key_weight, value_weight):
    group_count = nbr_rows.shape[0]
    normed = normalize(nbr_rows, enc_gain)
    flat_rows = normed.reshape(-1, normed.shape[-1])
    key_part = jnp.dot(flat_rows, key_weight, preferred_element_type=jnp.float32)
    value_part = jnp.dot(flat_rows, value_weight, preferred_element_type=jnp.float32)
    keys_out = key_part.astype(jnp.bfloat16)
    values_out = value_part.astype(jnp.bfloat16)
    return (
        keys_out.reshape(group_count, -1, keys_out.shape[-1]),
        values_out.reshape(group_count, -1, values_out.shape[-1]),
    )


def attend(grouped, keys_in, values_in):
    group_count = grouped.shape[0]
    query_heads = grouped.reshape(group_count, SPAN, HEADS, DH)
    key_heads = keys_in.reshape(group_count, -1, HEADS, DH)
    value_heads = values_in.reshape(group_count, -1, HEADS, DH)
    scores = jnp.einsum(
        "gqhd,gkhd->ghqk", query_heads, key_heads, preferred_element_type=jnp.float32
    ) * (1.0 / math.sqrt(DH))
    row_max = jnp.max(scores, axis=-1, keepdims=True)
    expo = jnp.exp(scores - row_max)
    probs_low = (expo / jnp.sum(expo, axis=-1, keepdims=True)).astype(jnp.bfloat16)
    mixed = jnp.einsum(
        "ghqk,gkhd->gqhd", probs_low, value_heads, preferred_element_type=jnp.float32
    )
    return mixed.reshape(group_count * SPAN, HEADS * DH).astype(jnp.bfloat16)


def body(queries, database, enc_gain, key_weight, value_weight, ret_shard, ret_row):
    spans = ret_shard.shape[0]
    nbr_count = ret_shard.shape[1]
    owners = lax.axis_size("seq")
    capacity = max(2, min(spans, 2 * spans * nbr_count // owners))
    requests = spans * nbr_count
    length = database.shape[1]
    enc_width = database.shape[2]
    shard_flat = ret_shard.reshape(requests)
    row_flat = ret_row.reshape(requests)
    order = jnp.arange(requests, dtype=jnp.int32)
    same_owner = shard_flat[:, None] == shard_flat[None, :]
    earlier = order[None, :] < order[:, None]
    slot_rank = jnp.sum(jnp.logical_and(same_owner, earlier), axis=1)
    owner_ids = jnp.arange(owners, dtype=jnp.int32)
    slot_ids = jnp.arange(capacity, dtype=jnp.int32)
    matches = jnp.logical_and(
        shard_flat[None, None, :] == owner_ids[:, None, None],
        slot_rank[None, None, :] == slot_ids[None, :, None],
    )
    wanted = jnp.sum(jnp.where(matches, row_flat[None, None, :] + 1, 0), axis=2) - 1
    wanted = jnp.broadcast_to(wanted[:, :, None], (owners, capacity, 128))
    wanted = jnp.pad(wanted, ((0, 0), (0, 8 - capacity), (0, 0)), constant_values=-1)
    table = database.reshape(database.shape[0] * length, enc_width)
    arrived, key_weight, value_weight = fetch(
        wanted, table, key_weight, value_weight, length, lax.axis_size("dp")
    )
    arrived = arrived.reshape(owners * capacity, length, enc_width)
    fetched = jnp.take(arrived, shard_flat * capacity + slot_rank, axis=0).reshape(
        spans, nbr_count, length, enc_width
    )
    prior_rows = from_behind(fetched[-1:], ("dp", "seq"), 1)
    keys_own, values_own = project(fetched, enc_gain, key_weight, value_weight)
    keys_prior, values_prior = project(prior_rows, enc_gain, key_weight, value_weight)
    keys_all = jnp.concatenate([keys_prior, keys_own], axis=0)
    values_all = jnp.concatenate([values_prior, values_own], axis=0)
    token_count = queries.shape[0]
    columns = queries.shape[1]
    padded = jnp.concatenate(
        [
            jnp.zeros((1, columns), queries.dtype),
            queries,
            jnp.zeros((SPAN - 1, columns), queries.dtype),
        ],
        axis=0,
    )
    grouped = padded.reshape(spans + 1, SPAN, columns)
    return attend(grouped, keys_all, values_all)[1 : 1 + token_count]


def solution(mesh):
    return jax.shard_map(
        body,
        mesh=mesh,
        in_specs=(
            P(("dp", "seq"), None),
            P("seq", None, None),
            P(),
            P(None, "dp"),
            P(None, "dp"),
            P(("dp", "seq"), None),
            P(("dp", "seq"), None),
        ),
        out_specs=P(("dp", "seq"), None),
        check_vma=False,
    )
```

```python
import functools
import math

import jax
import jax.numpy as jnp
from jax import lax
from jax.experimental import pallas as pl
from jax.experimental.pallas import tpu as pltpu
from jax.sharding import PartitionSpec as P

MESH = pl.DeviceIdType.MESH

HEADS = 16
DH = 128
SPAN = 64


eps_norm = 1e-06


def from_behind(block, axis, distance):
    devices = range(lax.axis_size(axis))
    route = [(i - distance, i) for i in devices if i - distance in devices]
    return lax.ppermute(block, axis, route)


def gathered_rows(ids_list, table_ref, length):
    pieces = []
    for ids in ids_list:
        for slot in range(2):
            pieces.append(jnp.broadcast_to(ids[slot : slot + 1, :], (length, 128)))
    sel = jnp.concatenate(pieces, axis=0)
    shape = sel.shape
    sub = lax.broadcasted_iota(jnp.int32, shape, 0)
    lane = lax.broadcasted_iota(jnp.int32, shape, 1)
    total = jnp.zeros((shape[0], table_ref.shape[1]), jnp.float32)
    for h in range(table_ref.shape[0] // 128):
        col = lane + h * 128
        hit = jnp.logical_and(col // length == sel, col % length == sub % length)
        total += jnp.dot(
            hit.astype(table_ref.dtype),
            table_ref[h * 128 : (h + 1) * 128, :],
            preferred_element_type=jnp.float32,
        )
    return total.astype(table_ref.dtype)


def torus_step(k, across, depth, sign):
    i = lax.rem(depth - k // across, depth)
    j = lax.rem(k, across)
    dz = sign * ((i + 1) // 2) * (2 * lax.rem(i, 2) - 1)
    dy = sign * ((j + 1) // 2) * (2 * lax.rem(j, 2) - 1)
    return dy, dz


def fetch_kernel(
    length, group, wanted_ref, table_ref, wk_ref, wv_ref, out_ref, wk_out, wv_out,
    asked, outgoing, req_send, req_recv, rep_send, rep_recv, wk_send, wk_recv, wv_send, wv_recv, own_sem,
):
    n = wanted_ref.shape[0]
    nd = wk_out.shape[1] // wk_ref.shape[1]
    me = lax.axis_index("seq")
    dp = lax.axis_index("dp")
    across = math.gcd(4, n)
    depth = n // across

    def peer_of(k, sign):
        dy, dz = torus_step(k, across, depth, sign)
        y = lax.rem(me, across)
        z = me // across
        return lax.rem(z + dz + depth, depth) * across + lax.rem(y + dy + across, across)

    def request(peer, slot):
        return pltpu.make_async_remote_copy(
            wanted_ref.at[peer], asked.at[slot], req_send.at[peer], req_recv.at[slot],
            device_id=(dp, peer), device_id_type=MESH,
        )

    def reply(step, peer, slot):
        return [
            pltpu.make_async_remote_copy(
                outgoing.at[step, pl.ds(half * length, length)],
                out_ref.at[slot, pl.ds(half * length, length)],
                rep_send.at[half, step], rep_recv.at[half, slot],
                device_id=(dp, peer), device_id_type=MESH,
            )
            for half in range(2)
        ]

    cols = wk_ref.shape[1]

    def weight(src, dst, send, recv, peer, slot):
        return pltpu.make_async_remote_copy(
            src, dst.at[:, pl.ds(slot * cols, cols)], send.at[peer], recv.at[slot],
            device_id=(peer, me), device_id_type=MESH,
        )

    def weights(peer, slot):
        return (
            weight(wk_ref, wk_out, wk_send, wk_recv, peer, slot),
            weight(wv_ref, wv_out, wv_send, wv_recv, peer, slot),
        )

    own = (
        pltpu.make_async_copy(wk_ref, wk_out.at[:, pl.ds(dp * cols, cols)], own_sem.at[0]),
        pltpu.make_async_copy(wv_ref, wv_out.at[:, pl.ds(dp * cols, cols)], own_sem.at[1]),
    )

    barrier = pltpu.get_barrier_semaphore()

    def greet(k, carry):
        pl.semaphore_signal(barrier, inc=1, device_id=(dp, lax.rem(me + k, n)), device_id_type=MESH)
        return carry

    def greet_dp(k, carry):
        pl.semaphore_signal(barrier, inc=1, device_id=(lax.rem(dp + k, nd), me), device_id_type=MESH)
        return carry

    lax.fori_loop(1, n, greet, 0)
    lax.fori_loop(1, nd, greet_dp, 0)
    pl.semaphore_wait(barrier, n - 1 + nd - 1)

    def share(k, carry):
        for copy in weights(lax.rem(dp + k, nd), dp):
            copy.start()
        return carry

    lax.fori_loop(1, nd, share, 0)
    for copy in own:
        copy.start()

    def ask(k, carry):
        request(peer_of(k, 1), me).start()
        return carry

    lax.fori_loop(1, n, ask, 0)

    asked[me] = wanted_ref[me]

    def serve(c, carry):
        ids_list = []
        for j in range(group):
            k = c * group + j
            source = peer_of(k, -1)

            @pl.when(k > 0)
            def _():
                request(source, source).wait_recv()

            ids_list.append(asked[source])
        rows = gathered_rows(ids_list, table_ref, length)
        outgoing[pl.ds(c * group, group)] = rows.reshape(group, 2 * length, rows.shape[-1])
        for j in range(group):
            k = c * group + j
            source = peer_of(k, -1)

            @pl.when(k == 0)
            def _():
                out_ref[me] = outgoing[k]

            @pl.when(k > 0)
            def _():
                for copy in reply(k, source, me):
                    copy.start()

        return carry

    lax.fori_loop(0, n // group, serve, 0)

    def finish(k, carry):
        peer = peer_of(k, 1)
        request(peer, me).wait_send()
        for copy in reply(k, peer_of(k, -1), me):
            copy.wait_send()
        for copy in reply(k, peer, peer):
            copy.wait_recv()
        return carry

    lax.fori_loop(1, n, finish, 0)

    def gathered(k, carry):
        peer = lax.rem(dp + k, nd)
        for copy in weights(peer, dp):
            copy.wait_send()
        for copy in weights(peer, peer):
            copy.wait_recv()
        return carry

    lax.fori_loop(1, nd, gathered, 0)
    for copy in own:
        copy.wait()


def fetch(wanted, table, key_weight, value_weight, length, nd):
    n = wanted.shape[0]
    width = table.shape[1]
    vmem = pl.BlockSpec(memory_space=pltpu.VMEM)
    anywhere = pl.BlockSpec(memory_space=pl.ANY)
    return pl.pallas_call(
        functools.partial(fetch_kernel, length, math.gcd(8, n)),
        out_shape=(
            jax.ShapeDtypeStruct((n, 2 * length, width), table.dtype),
            jax.ShapeDtypeStruct((key_weight.shape[0], nd * key_weight.shape[1]), key_weight.dtype),
            jax.ShapeDtypeStruct((value_weight.shape[0], nd * value_weight.shape[1]), value_weight.dtype),
        ),
        in_specs=[vmem, vmem, anywhere, anywhere],
        out_specs=(vmem, anywhere, anywhere),
        scratch_shapes=[
            pltpu.VMEM(wanted.shape, jnp.int32),
            pltpu.VMEM((n, 2 * length, width), table.dtype),
            pltpu.SemaphoreType.DMA((n,)),
            pltpu.SemaphoreType.DMA((n,)),
            pltpu.SemaphoreType.DMA((2, n)),
            pltpu.SemaphoreType.DMA((2, n)),
            pltpu.SemaphoreType.DMA((nd,)),
            pltpu.SemaphoreType.DMA((nd,)),
            pltpu.SemaphoreType.DMA((nd,)),
            pltpu.SemaphoreType.DMA((nd,)),
            pltpu.SemaphoreType.DMA((2,)),
        ],
        compiler_params=pltpu.CompilerParams(collective_id=0, has_side_effects=True),
    )(wanted, table, key_weight, value_weight)


def normalize(nbr_rows, enc_gain):
    widened = nbr_rows.astype(jnp.float32)
    mean_square = jnp.mean(widened * widened, axis=-1, keepdims=True)
    return (widened * lax.rsqrt(mean_square + eps_norm) * enc_gain).astype(jnp.bfloat16)


def project(nbr_rows, enc_gain, key_weight, value_weight):
    group_count = nbr_rows.shape[0]
    normed = normalize(nbr_rows, enc_gain)
    flat_rows = normed.reshape(-1, normed.shape[-1])
    key_part = jnp.dot(flat_rows, key_weight, preferred_element_type=jnp.float32)
    value_part = jnp.dot(flat_rows, value_weight, preferred_element_type=jnp.float32)
    keys_out = key_part.astype(jnp.bfloat16)
    values_out = value_part.astype(jnp.bfloat16)
    return (
        keys_out.reshape(group_count, -1, keys_out.shape[-1]),
        values_out.reshape(group_count, -1, values_out.shape[-1]),
    )


def attend(grouped, keys_in, values_in):
    group_count = grouped.shape[0]
    query_heads = grouped.reshape(group_count, SPAN, HEADS, DH)
    key_heads = keys_in.reshape(group_count, -1, HEADS, DH)
    value_heads = values_in.reshape(group_count, -1, HEADS, DH)
    scores = jnp.einsum(
        "gqhd,gkhd->ghqk", query_heads, key_heads, preferred_element_type=jnp.float32
    ) * (1.0 / math.sqrt(DH))
    row_max = jnp.max(scores, axis=-1, keepdims=True)
    expo = jnp.exp(scores - row_max)
    probs_low = (expo / jnp.sum(expo, axis=-1, keepdims=True)).astype(jnp.bfloat16)
    mixed = jnp.einsum(
        "ghqk,gkhd->gqhd", probs_low, value_heads, preferred_element_type=jnp.float32
    )
    return mixed.reshape(group_count * SPAN, HEADS * DH).astype(jnp.bfloat16)


def body(queries, database, enc_gain, key_weight, value_weight, ret_shard, ret_row):
    spans = ret_shard.shape[0]
    nbr_count = ret_shard.shape[1]
    owners = lax.axis_size("seq")
    capacity = max(2, min(spans, 2 * spans * nbr_count // owners))
    requests = spans * nbr_count
    length = database.shape[1]
    enc_width = database.shape[2]
    shard_flat = ret_shard.reshape(requests)
    row_flat = ret_row.reshape(requests)
    order = jnp.arange(requests, dtype=jnp.int32)
    same_owner = shard_flat[:, None] == shard_flat[None, :]
    earlier = order[None, :] < order[:, None]
    slot_rank = jnp.sum(jnp.logical_and(same_owner, earlier), axis=1)
    owner_ids = jnp.arange(owners, dtype=jnp.int32)
    slot_ids = jnp.arange(capacity, dtype=jnp.int32)
    matches = jnp.logical_and(
        shard_flat[None, None, :] == owner_ids[:, None, None],
        slot_rank[None, None, :] == slot_ids[None, :, None],
    )
    wanted = jnp.sum(jnp.where(matches, row_flat[None, None, :] + 1, 0), axis=2) - 1
    wanted = jnp.broadcast_to(wanted[:, :, None], (owners, capacity, 128))
    wanted = jnp.pad(wanted, ((0, 0), (0, 8 - capacity), (0, 0)), constant_values=-1)
    table = database.reshape(database.shape[0] * length, enc_width)
    arrived, key_weight, value_weight = fetch(
        wanted, table, key_weight, value_weight, length, lax.axis_size("dp")
    )
    arrived = arrived.reshape(owners * capacity, length, enc_width)
    fetched = jnp.take(arrived, shard_flat * capacity + slot_rank, axis=0).reshape(
        spans, nbr_count, length, enc_width
    )
    prior_rows = from_behind(fetched[-1:], ("dp", "seq"), 1)
    keys_own, values_own = project(fetched, enc_gain, key_weight, value_weight)
    keys_prior, values_prior = project(prior_rows, enc_gain, key_weight, value_weight)
    keys_all = jnp.concatenate([keys_prior, keys_own], axis=0)
    values_all = jnp.concatenate([values_prior, values_own], axis=0)
    token_count = queries.shape[0]
    columns = queries.shape[1]
    padded = jnp.concatenate(
        [
            jnp.zeros((1, columns), queries.dtype),
            queries,
            jnp.zeros((SPAN - 1, columns), queries.dtype),
        ],
        axis=0,
    )
    grouped = padded.reshape(spans + 1, SPAN, columns)
    return attend(grouped, keys_all, values_all)[1 : 1 + token_count]


def solution(mesh):
    return jax.shard_map(
        body,
        mesh=mesh,
        in_specs=(
            P(("dp", "seq"), None),
            P("seq", None, None),
            P(),
            P(None, "dp"),
            P(None, "dp"),
            P(("dp", "seq"), None),
            P(("dp", "seq"), None),
        ),
        out_specs=P(("dp", "seq"), None),
        check_vma=False,
    )
```

```python
import functools
import math

import jax
import jax.numpy as jnp
from jax import lax
from jax.experimental import pallas as pl
from jax.experimental.pallas import tpu as pltpu
from jax.sharding import PartitionSpec as P

MESH = pl.DeviceIdType.MESH

HEADS = 16
DH = 128
SPAN = 64


eps_norm = 1e-06


def from_behind(block, axis, distance):
    devices = range(lax.axis_size(axis))
    route = [(i - distance, i) for i in devices if i - distance in devices]
    return lax.ppermute(block, axis, route)


def gathered_rows(ids_list, table_ref, length):
    pieces = []
    for ids in ids_list:
        for slot in range(2):
            pieces.append(jnp.broadcast_to(ids[slot : slot + 1, :], (length, 128)))
    sel = jnp.concatenate(pieces, axis=0)
    shape = sel.shape
    sub = lax.broadcasted_iota(jnp.int32, shape, 0)
    lane = lax.broadcasted_iota(jnp.int32, shape, 1)
    total = jnp.zeros((shape[0], table_ref.shape[1]), jnp.float32)
    for h in range(table_ref.shape[0] // 128):
        col = lane + h * 128
        hit = jnp.logical_and(col // length == sel, col % length == sub % length)
        total += jnp.dot(
            hit.astype(table_ref.dtype),
            table_ref[h * 128 : (h + 1) * 128, :],
            preferred_element_type=jnp.float32,
        )
    return total.astype(table_ref.dtype)


def torus_step(k, across, depth, sign):
    i = lax.rem(depth - k // across, depth)
    j = lax.rem(k, across)
    dz = sign * ((i + 1) // 2) * (2 * lax.rem(i, 2) - 1)
    dy = sign * ((j + 1) // 2) * (2 * lax.rem(j, 2) - 1)
    return dy, dz


def fetch_kernel(
    length, group, wanted_ref, table_ref, wk_ref, wv_ref, out_ref, wk_out, wv_out,
    asked, outgoing, req_send, req_recv, rep_send, rep_recv, wk_send, wk_recv, wv_send, wv_recv, wk_fwd, wv_fwd,
    own_sem,
):
    n = wanted_ref.shape[0]
    nd = wk_out.shape[1] // wk_ref.shape[1]
    me = lax.axis_index("seq")
    dp = lax.axis_index("dp")
    across = math.gcd(4, n)
    depth = n // across

    def peer_of(k, sign):
        dy, dz = torus_step(k, across, depth, sign)
        y = lax.rem(me, across)
        z = me // across
        return lax.rem(z + dz + depth, depth) * across + lax.rem(y + dy + across, across)

    def request(peer, slot):
        return pltpu.make_async_remote_copy(
            wanted_ref.at[peer], asked.at[slot], req_send.at[peer], req_recv.at[slot],
            device_id=(dp, peer), device_id_type=MESH,
        )

    def reply(step, peer, slot):
        return pltpu.make_async_remote_copy(
            outgoing.at[step], out_ref.at[slot], rep_send.at[step], rep_recv.at[slot],
            device_id=(dp, peer), device_id_type=MESH,
        )

    cols = wk_ref.shape[1]
    partner = dp + 1 - 2 * lax.rem(dp, 2)
    pairs = nd // 2

    def weights(src_k, src_v, peer, slot, sent_k, sent_v, sent_slot):
        return [
            pltpu.make_async_remote_copy(
                src, dst.at[:, pl.ds(slot * cols, cols)], sent.at[sent_slot], recv.at[slot],
                device_id=(peer, me), device_id_type=MESH,
            )
            for src, dst, sent, recv in ((src_k, wk_out, sent_k, wk_recv), (src_v, wv_out, sent_v, wv_recv))
        ]

    def own_shard(peer):
        return weights(wk_ref, wv_ref, peer, dp, wk_send, wv_send, peer)

    def relayed(slot, peer):
        return weights(
            wk_out.at[:, pl.ds(slot * cols, cols)], wv_out.at[:, pl.ds(slot * cols, cols)],
            peer, slot, wk_fwd, wv_fwd, slot,
        )

    own = (
        pltpu.make_async_copy(wk_ref, wk_out.at[:, pl.ds(dp * cols, cols)], own_sem.at[0]),
        pltpu.make_async_copy(wv_ref, wv_out.at[:, pl.ds(dp * cols, cols)], own_sem.at[1]),
    )

    barrier = pltpu.get_barrier_semaphore()

    def greet(k, carry):
        pl.semaphore_signal(barrier, inc=1, device_id=(dp, lax.rem(me + k, n)), device_id_type=MESH)
        return carry

    def greet_dp(k, carry):
        pl.semaphore_signal(barrier, inc=1, device_id=(lax.rem(dp + k, nd), me), device_id_type=MESH)
        return carry

    lax.fori_loop(1, n, greet, 0)
    lax.fori_loop(1, nd, greet_dp, 0)
    pl.semaphore_wait(barrier, n - 1 + nd - 1)

    def share(m, carry):
        for copy in own_shard(lax.rem(dp + 2 * m, nd)):
            copy.start()
        return carry

    for copy in own_shard(partner):
        copy.start()
    lax.fori_loop(1, pairs, share, 0)
    for copy in own:
        copy.start()

    def ask(k, carry):
        request(peer_of(k, 1), me).start()
        return carry

    lax.fori_loop(1, n, ask, 0)

    asked[me] = wanted_ref[me]

    def serve(c, carry):
        ids_list = []
        for j in range(group):
            k = c * group + j
            source = peer_of(k, -1)

            @pl.when(k > 0)
            def _():
                request(source, source).wait_recv()

            ids_list.append(asked[source])
        rows = gathered_rows(ids_list, table_ref, length)
        outgoing[pl.ds(c * group, group)] = rows.reshape(group, 2 * length, rows.shape[-1])
        for j in range(group):
            k = c * group + j
            source = peer_of(k, -1)

            @pl.when(k == 0)
            def _():
                out_ref[me] = outgoing[k]

            @pl.when(k > 0)
            def _():
                reply(k, source, me).start()

        return carry

    lax.fori_loop(0, n // group, serve, 0)

    def relay(m, carry):
        slot = lax.rem(dp + 2 * m, nd)
        for copy in relayed(slot, partner):
            copy.wait_recv()
        for copy in relayed(slot, partner):
            copy.start()
        return carry

    lax.fori_loop(1, pairs, relay, 0)

    def finish(k, carry):
        peer = peer_of(k, 1)
        request(peer, me).wait_send()
        reply(k, peer_of(k, -1), me).wait_send()
        reply(k, peer, peer).wait_recv()
        return carry

    lax.fori_loop(1, n, finish, 0)

    def gathered(m, carry):
        peer = lax.rem(dp + 2 * m, nd)
        for copy in own_shard(peer):
            copy.wait_send()
        for copy in relayed(peer, partner):
            copy.wait_send()
        for copy in relayed(lax.rem(partner + 2 * m, nd), partner):
            copy.wait_recv()
        return carry

    lax.fori_loop(1, pairs, gathered, 0)
    for copy in own_shard(partner):
        copy.wait_send()
    for copy in relayed(partner, partner):
        copy.wait_recv()
    for copy in own:
        copy.wait()


def fetch(wanted, table, key_weight, value_weight, length, nd):
    n = wanted.shape[0]
    width = table.shape[1]
    vmem = pl.BlockSpec(memory_space=pltpu.VMEM)
    anywhere = pl.BlockSpec(memory_space=pl.ANY)
    return pl.pallas_call(
        functools.partial(fetch_kernel, length, math.gcd(8, n)),
        out_shape=(
            jax.ShapeDtypeStruct((n, 2 * length, width), table.dtype),
            jax.ShapeDtypeStruct((key_weight.shape[0], nd * key_weight.shape[1]), key_weight.dtype),
            jax.ShapeDtypeStruct((value_weight.shape[0], nd * value_weight.shape[1]), value_weight.dtype),
        ),
        in_specs=[vmem, vmem, anywhere, anywhere],
        out_specs=(vmem, anywhere, anywhere),
        scratch_shapes=[
            pltpu.VMEM(wanted.shape, jnp.int32),
            pltpu.VMEM((n, 2 * length, width), table.dtype),
            pltpu.SemaphoreType.DMA((n,)),
            pltpu.SemaphoreType.DMA((n,)),
            pltpu.SemaphoreType.DMA((n,)),
            pltpu.SemaphoreType.DMA((n,)),
            pltpu.SemaphoreType.DMA((nd,)),
            pltpu.SemaphoreType.DMA((nd,)),
            pltpu.SemaphoreType.DMA((nd,)),
            pltpu.SemaphoreType.DMA((nd,)),
            pltpu.SemaphoreType.DMA((nd,)),
            pltpu.SemaphoreType.DMA((nd,)),
            pltpu.SemaphoreType.DMA((2,)),
        ],
        compiler_params=pltpu.CompilerParams(collective_id=0, has_side_effects=True),
    )(wanted, table, key_weight, value_weight)


def normalize(nbr_rows, enc_gain):
    widened = nbr_rows.astype(jnp.float32)
    mean_square = jnp.mean(widened * widened, axis=-1, keepdims=True)
    return (widened * lax.rsqrt(mean_square + eps_norm) * enc_gain).astype(jnp.bfloat16)


def project(nbr_rows, enc_gain, key_weight, value_weight):
    group_count = nbr_rows.shape[0]
    normed = normalize(nbr_rows, enc_gain)
    flat_rows = normed.reshape(-1, normed.shape[-1])
    key_part = jnp.dot(flat_rows, key_weight, preferred_element_type=jnp.float32)
    value_part = jnp.dot(flat_rows, value_weight, preferred_element_type=jnp.float32)
    keys_out = key_part.astype(jnp.bfloat16)
    values_out = value_part.astype(jnp.bfloat16)
    return (
        keys_out.reshape(group_count, -1, keys_out.shape[-1]),
        values_out.reshape(group_count, -1, values_out.shape[-1]),
    )


def attend(grouped, keys_in, values_in):
    group_count = grouped.shape[0]
    query_heads = grouped.reshape(group_count, SPAN, HEADS, DH)
    key_heads = keys_in.reshape(group_count, -1, HEADS, DH)
    value_heads = values_in.reshape(group_count, -1, HEADS, DH)
    scores = jnp.einsum(
        "gqhd,gkhd->ghqk", query_heads, key_heads, preferred_element_type=jnp.float32
    ) * (1.0 / math.sqrt(DH))
    row_max = jnp.max(scores, axis=-1, keepdims=True)
    expo = jnp.exp(scores - row_max)
    probs_low = (expo / jnp.sum(expo, axis=-1, keepdims=True)).astype(jnp.bfloat16)
    mixed = jnp.einsum(
        "ghqk,gkhd->gqhd", probs_low, value_heads, preferred_element_type=jnp.float32
    )
    return mixed.reshape(group_count * SPAN, HEADS * DH).astype(jnp.bfloat16)


def body(queries, database, enc_gain, key_weight, value_weight, ret_shard, ret_row):
    spans = ret_shard.shape[0]
    nbr_count = ret_shard.shape[1]
    owners = lax.axis_size("seq")
    capacity = max(2, min(spans, 2 * spans * nbr_count // owners))
    requests = spans * nbr_count
    length = database.shape[1]
    enc_width = database.shape[2]
    shard_flat = ret_shard.reshape(requests)
    row_flat = ret_row.reshape(requests)
    order = jnp.arange(requests, dtype=jnp.int32)
    same_owner = shard_flat[:, None] == shard_flat[None, :]
    earlier = order[None, :] < order[:, None]
    slot_rank = jnp.sum(jnp.logical_and(same_owner, earlier), axis=1)
    owner_ids = jnp.arange(owners, dtype=jnp.int32)
    slot_ids = jnp.arange(capacity, dtype=jnp.int32)
    matches = jnp.logical_and(
        shard_flat[None, None, :] == owner_ids[:, None, None],
        slot_rank[None, None, :] == slot_ids[None, :, None],
    )
    wanted = jnp.sum(jnp.where(matches, row_flat[None, None, :] + 1, 0), axis=2) - 1
    wanted = jnp.broadcast_to(wanted[:, :, None], (owners, capacity, 128))
    wanted = jnp.pad(wanted, ((0, 0), (0, 8 - capacity), (0, 0)), constant_values=-1)
    table = database.reshape(database.shape[0] * length, enc_width)
    arrived, key_weight, value_weight = fetch(
        wanted, table, key_weight, value_weight, length, lax.axis_size("dp")
    )
    arrived = arrived.reshape(owners * capacity, length, enc_width)
    fetched = jnp.take(arrived, shard_flat * capacity + slot_rank, axis=0).reshape(
        spans, nbr_count, length, enc_width
    )
    prior_rows = from_behind(fetched[-1:], ("dp", "seq"), 1)
    keys_own, values_own = project(fetched, enc_gain, key_weight, value_weight)
    keys_prior, values_prior = project(prior_rows, enc_gain, key_weight, value_weight)
    keys_all = jnp.concatenate([keys_prior, keys_own], axis=0)
    values_all = jnp.concatenate([values_prior, values_own], axis=0)
    token_count = queries.shape[0]
    columns = queries.shape[1]
    padded = jnp.concatenate(
        [
            jnp.zeros((1, columns), queries.dtype),
            queries,
            jnp.zeros((SPAN - 1, columns), queries.dtype),
        ],
        axis=0,
    )
    grouped = padded.reshape(spans + 1, SPAN, columns)
    return attend(grouped, keys_all, values_all)[1 : 1 + token_count]


def solution(mesh):
    return jax.shard_map(
        body,
        mesh=mesh,
        in_specs=(
            P(("dp", "seq"), None),
            P("seq", None, None),
            P(),
            P(None, "dp"),
            P(None, "dp"),
            P(("dp", "seq"), None),
            P(("dp", "seq"), None),
        ),
        out_specs=P(("dp", "seq"), None),
        check_vma=False,
    )
```

```python
import functools
import math

import jax
import jax.numpy as jnp
from jax import lax
from jax.experimental import pallas as pl
from jax.experimental.pallas import tpu as pltpu
from jax.sharding import PartitionSpec as P

MESH = pl.DeviceIdType.MESH

HEADS = 16
DH = 128
SPAN = 64


eps_norm = 1e-06


def from_behind(block, axis, distance):
    devices = range(lax.axis_size(axis))
    route = [(i - distance, i) for i in devices if i - distance in devices]
    return lax.ppermute(block, axis, route)


def gathered_rows(ids_list, table_ref, length):
    pieces = []
    for ids in ids_list:
        for slot in range(2):
            pieces.append(jnp.broadcast_to(ids[slot : slot + 1, :], (length, 128)))
    sel = jnp.concatenate(pieces, axis=0)
    shape = sel.shape
    sub = lax.broadcasted_iota(jnp.int32, shape, 0)
    lane = lax.broadcasted_iota(jnp.int32, shape, 1)
    total = jnp.zeros((shape[0], table_ref.shape[1]), jnp.float32)
    for h in range(table_ref.shape[0] // 128):
        col = lane + h * 128
        hit = jnp.logical_and(col // length == sel, col % length == sub % length)
        total += jnp.dot(
            hit.astype(table_ref.dtype),
            table_ref[h * 128 : (h + 1) * 128, :],
            preferred_element_type=jnp.float32,
        )
    return total.astype(table_ref.dtype)


def torus_step(k, across, depth, sign):
    i = lax.rem(depth - k // across, depth)
    j = lax.rem(k, across)
    dz = sign * ((i + 1) // 2) * (2 * lax.rem(i, 2) - 1)
    dy = sign * ((j + 1) // 2) * (2 * lax.rem(j, 2) - 1)
    return dy, dz


def fetch_kernel(
    length, group, wanted_ref, table_ref, wk_ref, wv_ref, out_ref, wk_out, wv_out,
    asked, outgoing, req_send, req_recv, rep_send, rep_recv, wk_send, wk_recv, wv_send, wv_recv, own_sem,
):
    n = wanted_ref.shape[0]
    nd = wk_out.shape[1] // wk_ref.shape[1]
    me = lax.axis_index("seq")
    dp = lax.axis_index("dp")
    across = math.gcd(4, n)
    depth = n // across

    def peer_of(k, sign):
        dy, dz = torus_step(k, across, depth, sign)
        y = lax.rem(me, across)
        z = me // across
        return lax.rem(z + dz + depth, depth) * across + lax.rem(y + dy + across, across)

    def request(peer, slot):
        return pltpu.make_async_remote_copy(
            wanted_ref.at[peer], asked.at[slot], req_send.at[peer], req_recv.at[slot],
            device_id=(dp, peer), device_id_type=MESH,
        )

    def reply(step, peer, slot):
        return pltpu.make_async_remote_copy(
            outgoing.at[step], out_ref.at[slot], rep_send.at[step], rep_recv.at[slot],
            device_id=(dp, peer), device_id_type=MESH,
        )

    cols = wk_ref.shape[1]

    def weight(src, dst, send, recv, peer, slot):
        return pltpu.make_async_remote_copy(
            src, dst.at[:, pl.ds(slot * cols, cols)], send.at[peer], recv.at[slot],
            device_id=(peer, me), device_id_type=MESH,
        )

    def weights(peer, slot):
        return (
            weight(wk_ref, wk_out, wk_send, wk_recv, peer, slot),
            weight(wv_ref, wv_out, wv_send, wv_recv, peer, slot),
        )

    own = (
        pltpu.make_async_copy(wk_ref, wk_out.at[:, pl.ds(dp * cols, cols)], own_sem.at[0]),
        pltpu.make_async_copy(wv_ref, wv_out.at[:, pl.ds(dp * cols, cols)], own_sem.at[1]),
    )

    barrier = pltpu.get_barrier_semaphore()

    def greet(k, carry):
        pl.semaphore_signal(barrier, inc=1, device_id=(dp, lax.rem(me + k, n)), device_id_type=MESH)
        return carry

    def greet_dp(k, carry):
        pl.semaphore_signal(barrier, inc=1, device_id=(lax.rem(dp + k, nd), me), device_id_type=MESH)
        return carry

    lax.fori_loop(1, n, greet, 0)
    lax.fori_loop(1, nd, greet_dp, 0)
    pl.semaphore_wait(barrier, n - 1 + nd - 1)

    def share(k, carry):
        for copy in weights(lax.rem(dp + k, nd), dp):
            copy.start()
        return carry

    lax.fori_loop(1, nd, share, 0)
    for copy in own:
        copy.start()

    def ask(k, carry):
        request(peer_of(k, 1), me).start()
        return carry

    lax.fori_loop(1, n, ask, 0)

    asked[me] = wanted_ref[me]

    def serve(c, carry):
        ids_list = []
        for j in range(group):
            k = c * group + j
            source = peer_of(k, -1)

            @pl.when(k > 0)
            def _():
                request(source, source).wait_recv()

            ids_list.append(asked[source])
        rows = gathered_rows(ids_list, table_ref, length)
        outgoing[pl.ds(c * group, group)] = rows.reshape(group, 2 * length, rows.shape[-1])
        for j in range(group):
            k = c * group + j
            source = peer_of(k, -1)

            @pl.when(k == 0)
            def _():
                out_ref[me] = outgoing[k]

            @pl.when(k > 0)
            def _():
                reply(k, source, me).start()

        return carry

    lax.fori_loop(0, n // group, serve, 0)

    def finish(k, carry):
        peer = peer_of(k, 1)
        request(peer, me).wait_send()
        reply(k, peer_of(k, -1), me).wait_send()
        reply(k, peer, peer).wait_recv()
        return carry

    lax.fori_loop(1, n, finish, 0)

    def gathered(k, carry):
        peer = lax.rem(dp + k, nd)
        for copy in weights(peer, dp):
            copy.wait_send()
        for copy in weights(peer, peer):
            copy.wait_recv()
        return carry

    lax.fori_loop(1, nd, gathered, 0)
    for copy in own:
        copy.wait()


def fetch(wanted, table, key_weight, value_weight, length, nd):
    n = wanted.shape[0]
    width = table.shape[1]
    vmem = pl.BlockSpec(memory_space=pltpu.VMEM)
    anywhere = pl.BlockSpec(memory_space=pl.ANY)
    return pl.pallas_call(
        functools.partial(fetch_kernel, length, math.gcd(8, n)),
        out_shape=(
            jax.ShapeDtypeStruct((n, 2 * length, width), table.dtype),
            jax.ShapeDtypeStruct((key_weight.shape[0], nd * key_weight.shape[1]), key_weight.dtype),
            jax.ShapeDtypeStruct((value_weight.shape[0], nd * value_weight.shape[1]), value_weight.dtype),
        ),
        in_specs=[vmem, vmem, anywhere, anywhere],
        out_specs=(vmem, anywhere, anywhere),
        scratch_shapes=[
            pltpu.VMEM(wanted.shape, jnp.int32),
            pltpu.VMEM((n, 2 * length, width), table.dtype),
            pltpu.SemaphoreType.DMA((n,)),
            pltpu.SemaphoreType.DMA((n,)),
            pltpu.SemaphoreType.DMA((n,)),
            pltpu.SemaphoreType.DMA((n,)),
            pltpu.SemaphoreType.DMA((nd,)),
            pltpu.SemaphoreType.DMA((nd,)),
            pltpu.SemaphoreType.DMA((nd,)),
            pltpu.SemaphoreType.DMA((nd,)),
            pltpu.SemaphoreType.DMA((2,)),
        ],
        compiler_params=pltpu.CompilerParams(collective_id=0, has_side_effects=True),
    )(wanted, table, key_weight, value_weight)


def normalize(nbr_rows, enc_gain):
    widened = nbr_rows.astype(jnp.float32)
    mean_square = jnp.mean(widened * widened, axis=-1, keepdims=True)
    return (widened * lax.rsqrt(mean_square + eps_norm) * enc_gain).astype(jnp.bfloat16)


def project(nbr_rows, enc_gain, key_weight, value_weight):
    group_count = nbr_rows.shape[0]
    normed = normalize(nbr_rows, enc_gain)
    flat_rows = normed.reshape(-1, normed.shape[-1])
    key_part = jnp.dot(flat_rows, key_weight, preferred_element_type=jnp.float32)
    value_part = jnp.dot(flat_rows, value_weight, preferred_element_type=jnp.float32)
    keys_out = key_part.astype(jnp.bfloat16)
    values_out = value_part.astype(jnp.bfloat16)
    return (
        keys_out.reshape(group_count, -1, keys_out.shape[-1]),
        values_out.reshape(group_count, -1, values_out.shape[-1]),
    )


def attend(grouped, keys_in, values_in):
    group_count = grouped.shape[0]
    query_heads = grouped.reshape(group_count, SPAN, HEADS, DH)
    key_heads = keys_in.reshape(group_count, -1, HEADS, DH)
    value_heads = values_in.reshape(group_count, -1, HEADS, DH)
    scores = jnp.einsum(
        "gqhd,gkhd->ghqk", query_heads, key_heads, preferred_element_type=jnp.float32
    ) * (1.0 / math.sqrt(DH))
    row_max = jnp.max(scores, axis=-1, keepdims=True)
    expo = jnp.exp(scores - row_max)
    probs_low = (expo / jnp.sum(expo, axis=-1, keepdims=True)).astype(jnp.bfloat16)
    mixed = jnp.einsum(
        "ghqk,gkhd->gqhd", probs_low, value_heads, preferred_element_type=jnp.float32
    )
    return mixed.reshape(group_count * SPAN, HEADS * DH).astype(jnp.bfloat16)


def body(queries, database, enc_gain, key_weight, value_weight, ret_shard, ret_row):
    spans = ret_shard.shape[0]
    nbr_count = ret_shard.shape[1]
    owners = lax.axis_size("seq")
    capacity = max(2, min(spans, 2 * spans * nbr_count // owners))
    requests = spans * nbr_count
    length = database.shape[1]
    enc_width = database.shape[2]
    shard_flat = ret_shard.reshape(requests)
    row_flat = ret_row.reshape(requests)
    order = jnp.arange(requests, dtype=jnp.int32)
    same_owner = shard_flat[:, None] == shard_flat[None, :]
    earlier = order[None, :] < order[:, None]
    slot_rank = jnp.sum(jnp.logical_and(same_owner, earlier), axis=1)
    owner_ids = jnp.arange(owners, dtype=jnp.int32)
    slot_ids = jnp.arange(capacity, dtype=jnp.int32)
    matches = jnp.logical_and(
        shard_flat[None, None, :] == owner_ids[:, None, None],
        slot_rank[None, None, :] == slot_ids[None, :, None],
    )
    wanted = jnp.sum(jnp.where(matches, row_flat[None, None, :] + 1, 0), axis=2) - 1
    wanted = jnp.broadcast_to(wanted[:, :, None], (owners, capacity, 128))
    wanted = jnp.pad(wanted, ((0, 0), (0, 8 - capacity), (0, 0)), constant_values=-1)
    table = database.reshape(database.shape[0] * length, enc_width)
    arrived, key_weight, value_weight = fetch(
        wanted, table, key_weight, value_weight, length, lax.axis_size("dp")
    )
    arrived = arrived.reshape(owners * capacity, length, enc_width)
    fetched = jnp.take(arrived, shard_flat * capacity + slot_rank, axis=0).reshape(
        spans, nbr_count, length, enc_width
    )
    last_slots = (shard_flat * capacity + slot_rank)[requests - nbr_count :]
    last_rows = jnp.take(arrived, last_slots, axis=0)[None]
    prior_rows = from_behind(last_rows, ("dp", "seq"), 1)
    keys_own, values_own = project(fetched, enc_gain, key_weight, value_weight)
    keys_prior, values_prior = project(prior_rows, enc_gain, key_weight, value_weight)
    keys_all = jnp.concatenate([keys_prior, keys_own], axis=0)
    values_all = jnp.concatenate([values_prior, values_own], axis=0)
    token_count = queries.shape[0]
    columns = queries.shape[1]
    padded = jnp.concatenate(
        [
            jnp.zeros((1, columns), queries.dtype),
            queries,
            jnp.zeros((SPAN - 1, columns), queries.dtype),
        ],
        axis=0,
    )
    grouped = padded.reshape(spans + 1, SPAN, columns)
    return attend(grouped, keys_all, values_all)[1 : 1 + token_count]


def solution(mesh):
    return jax.shard_map(
        body,
        mesh=mesh,
        in_specs=(
            P(("dp", "seq"), None),
            P("seq", None, None),
            P(),
            P(None, "dp"),
            P(None, "dp"),
            P(("dp", "seq"), None),
            P(("dp", "seq"), None),
        ),
        out_specs=P(("dp", "seq"), None),
        check_vma=False,
    )
```

```python
import functools
import math

import jax
import jax.numpy as jnp
from jax import lax
from jax.experimental import pallas as pl
from jax.experimental.pallas import tpu as pltpu
from jax.sharding import PartitionSpec as P

MESH = pl.DeviceIdType.MESH

HEADS = 16
DH = 128
SPAN = 64


eps_norm = 1e-06


def from_behind(block, axis, distance):
    devices = range(lax.axis_size(axis))
    route = [(i - distance, i) for i in devices if i - distance in devices]
    return lax.ppermute(block, axis, route)


def gathered_rows(ids_list, table_ref, length):
    pieces = []
    for ids in ids_list:
        for slot in range(2):
            pieces.append(jnp.broadcast_to(ids[slot : slot + 1, :], (length, 128)))
    sel = jnp.concatenate(pieces, axis=0)
    shape = sel.shape
    sub = lax.broadcasted_iota(jnp.int32, shape, 0)
    lane = lax.broadcasted_iota(jnp.int32, shape, 1)
    total = jnp.zeros((shape[0], table_ref.shape[1]), jnp.float32)
    for h in range(table_ref.shape[0] // 128):
        col = lane + h * 128
        hit = jnp.logical_and(col // length == sel, col % length == sub % length)
        total += jnp.dot(
            hit.astype(table_ref.dtype),
            table_ref[h * 128 : (h + 1) * 128, :],
            preferred_element_type=jnp.float32,
        )
    return total.astype(table_ref.dtype)


def torus_step(k, across, depth, sign):
    i = lax.rem(depth - k // across, depth)
    j = lax.rem(k, across)
    dz = sign * ((i + 1) // 2) * (2 * lax.rem(i, 2) - 1)
    dy = sign * ((j + 1) // 2) * (2 * lax.rem(j, 2) - 1)
    return dy, dz


def fetch_kernel(
    length, group, wanted_ref, table_ref, wk_ref, wv_ref, out_ref, wk_out, wv_out,
    asked, outgoing, req_send, req_recv, rep_send, rep_recv, wk_send, wk_recv, wv_send, wv_recv, own_sem,
):
    n = wanted_ref.shape[0]
    nd = wk_out.shape[1] // wk_ref.shape[1]
    me = lax.axis_index("seq")
    dp = lax.axis_index("dp")
    across = math.gcd(4, n)
    depth = n // across

    def peer_of(k, sign):
        dy, dz = torus_step(k, across, depth, sign)
        y = lax.rem(me, across)
        z = me // across
        return lax.rem(z + dz + depth, depth) * across + lax.rem(y + dy + across, across)

    def request(peer, slot):
        return pltpu.make_async_remote_copy(
            wanted_ref.at[peer], asked.at[slot], req_send.at[peer], req_recv.at[slot],
            device_id=(dp, peer), device_id_type=MESH,
        )

    def reply(step, peer, slot):
        return pltpu.make_async_remote_copy(
            outgoing.at[step], out_ref.at[slot], rep_send.at[step], rep_recv.at[slot],
            device_id=(dp, peer), device_id_type=MESH,
        )

    cols = wk_ref.shape[1]

    def weight(src, dst, send, recv, peer, slot):
        return pltpu.make_async_remote_copy(
            src, dst.at[:, pl.ds(slot * cols, cols)], send.at[peer], recv.at[slot],
            device_id=(peer, me), device_id_type=MESH,
        )

    def weights(peer, slot):
        return (
            weight(wk_ref, wk_out, wk_send, wk_recv, peer, slot),
            weight(wv_ref, wv_out, wv_send, wv_recv, peer, slot),
        )

    own = (
        pltpu.make_async_copy(wk_ref, wk_out.at[:, pl.ds(dp * cols, cols)], own_sem.at[0]),
        pltpu.make_async_copy(wv_ref, wv_out.at[:, pl.ds(dp * cols, cols)], own_sem.at[1]),
    )

    barrier = pltpu.get_barrier_semaphore()

    def greet(k, carry):
        pl.semaphore_signal(barrier, inc=1, device_id=(dp, lax.rem(me + k, n)), device_id_type=MESH)
        return carry

    def greet_dp(k, carry):
        pl.semaphore_signal(barrier, inc=1, device_id=(lax.rem(dp + k, nd), me), device_id_type=MESH)
        return carry

    lax.fori_loop(1, n, greet, 0)
    lax.fori_loop(1, nd, greet_dp, 0)
    pl.semaphore_wait(barrier, n - 1 + nd - 1)

    def share(k, carry):
        for copy in weights(lax.rem(dp + k, nd), dp):
            copy.start()
        return carry

    lax.fori_loop(1, nd, share, 0)
    for copy in own:
        copy.start()

    def ask(k, carry):
        request(peer_of(k, 1), me).start()
        return carry

    lax.fori_loop(1, n, ask, 0)

    asked[me] = wanted_ref[me]

    def serve(c, carry):
        ids_list = []
        for j in range(group):
            k = c * group + j
            source = peer_of(k, -1)

            @pl.when(k > 0)
            def _():
                request(source, source).wait_recv()

            ids_list.append(asked[source])
        rows = gathered_rows(ids_list, table_ref, length)
        outgoing[pl.ds(c * group, group)] = rows.reshape(group, 2 * length, rows.shape[-1])
        for j in range(group):
            k = c * group + j
            source = peer_of(k, -1)

            @pl.when(k == 0)
            def _():
                pltpu.make_async_copy(outgoing.at[k], out_ref.at[me], own_sem.at[2]).start()

            @pl.when(k > 0)
            def _():
                reply(k, source, me).start()

        return carry

    lax.fori_loop(0, n // group, serve, 0)

    def finish(k, carry):
        peer = peer_of(k, 1)
        request(peer, me).wait_send()
        reply(k, peer_of(k, -1), me).wait_send()
        reply(k, peer, peer).wait_recv()
        return carry

    lax.fori_loop(1, n, finish, 0)

    def gathered(k, carry):
        peer = lax.rem(dp + k, nd)
        for copy in weights(peer, dp):
            copy.wait_send()
        for copy in weights(peer, peer):
            copy.wait_recv()
        return carry

    lax.fori_loop(1, nd, gathered, 0)
    for copy in own:
        copy.wait()
    pltpu.make_async_copy(outgoing.at[0], out_ref.at[me], own_sem.at[2]).wait()


def fetch(wanted, table, key_weight, value_weight, length, nd):
    n = wanted.shape[0]
    width = table.shape[1]
    vmem = pl.BlockSpec(memory_space=pltpu.VMEM)
    anywhere = pl.BlockSpec(memory_space=pl.ANY)
    return pl.pallas_call(
        functools.partial(fetch_kernel, length, math.gcd(8, n)),
        out_shape=(
            jax.ShapeDtypeStruct((n, 2 * length, width), table.dtype),
            jax.ShapeDtypeStruct((key_weight.shape[0], nd * key_weight.shape[1]), key_weight.dtype),
            jax.ShapeDtypeStruct((value_weight.shape[0], nd * value_weight.shape[1]), value_weight.dtype),
        ),
        in_specs=[vmem, vmem, anywhere, anywhere],
        out_specs=(anywhere, anywhere, anywhere),
        scratch_shapes=[
            pltpu.VMEM(wanted.shape, jnp.int32),
            pltpu.VMEM((n, 2 * length, width), table.dtype),
            pltpu.SemaphoreType.DMA((n,)),
            pltpu.SemaphoreType.DMA((n,)),
            pltpu.SemaphoreType.DMA((n,)),
            pltpu.SemaphoreType.DMA((n,)),
            pltpu.SemaphoreType.DMA((nd,)),
            pltpu.SemaphoreType.DMA((nd,)),
            pltpu.SemaphoreType.DMA((nd,)),
            pltpu.SemaphoreType.DMA((nd,)),
            pltpu.SemaphoreType.DMA((3,)),
        ],
        compiler_params=pltpu.CompilerParams(collective_id=0, has_side_effects=True),
    )(wanted, table, key_weight, value_weight)


def normalize(nbr_rows, enc_gain):
    widened = nbr_rows.astype(jnp.float32)
    mean_square = jnp.mean(widened * widened, axis=-1, keepdims=True)
    return (widened * lax.rsqrt(mean_square + eps_norm) * enc_gain).astype(jnp.bfloat16)


def project(nbr_rows, enc_gain, key_weight, value_weight):
    group_count = nbr_rows.shape[0]
    normed = normalize(nbr_rows, enc_gain)
    flat_rows = normed.reshape(-1, normed.shape[-1])
    key_part = jnp.dot(flat_rows, key_weight, preferred_element_type=jnp.float32)
    value_part = jnp.dot(flat_rows, value_weight, preferred_element_type=jnp.float32)
    keys_out = key_part.astype(jnp.bfloat16)
    values_out = value_part.astype(jnp.bfloat16)
    return (
        keys_out.reshape(group_count, -1, keys_out.shape[-1]),
        values_out.reshape(group_count, -1, values_out.shape[-1]),
    )


def attend(grouped, keys_in, values_in):
    group_count = grouped.shape[0]
    query_heads = grouped.reshape(group_count, SPAN, HEADS, DH)
    key_heads = keys_in.reshape(group_count, -1, HEADS, DH)
    value_heads = values_in.reshape(group_count, -1, HEADS, DH)
    scores = jnp.einsum(
        "gqhd,gkhd->ghqk", query_heads, key_heads, preferred_element_type=jnp.float32
    ) * (1.0 / math.sqrt(DH))
    row_max = jnp.max(scores, axis=-1, keepdims=True)
    expo = jnp.exp(scores - row_max)
    probs_low = (expo / jnp.sum(expo, axis=-1, keepdims=True)).astype(jnp.bfloat16)
    mixed = jnp.einsum(
        "ghqk,gkhd->gqhd", probs_low, value_heads, preferred_element_type=jnp.float32
    )
    return mixed.reshape(group_count * SPAN, HEADS * DH).astype(jnp.bfloat16)


def body(queries, database, enc_gain, key_weight, value_weight, ret_shard, ret_row):
    spans = ret_shard.shape[0]
    nbr_count = ret_shard.shape[1]
    owners = lax.axis_size("seq")
    capacity = max(2, min(spans, 2 * spans * nbr_count // owners))
    requests = spans * nbr_count
    length = database.shape[1]
    enc_width = database.shape[2]
    shard_flat = ret_shard.reshape(requests)
    row_flat = ret_row.reshape(requests)
    order = jnp.arange(requests, dtype=jnp.int32)
    same_owner = shard_flat[:, None] == shard_flat[None, :]
    earlier = order[None, :] < order[:, None]
    slot_rank = jnp.sum(jnp.logical_and(same_owner, earlier), axis=1)
    owner_ids = jnp.arange(owners, dtype=jnp.int32)
    slot_ids = jnp.arange(capacity, dtype=jnp.int32)
    matches = jnp.logical_and(
        shard_flat[None, None, :] == owner_ids[:, None, None],
        slot_rank[None, None, :] == slot_ids[None, :, None],
    )
    wanted = jnp.sum(jnp.where(matches, row_flat[None, None, :] + 1, 0), axis=2) - 1
    wanted = jnp.broadcast_to(wanted[:, :, None], (owners, capacity, 128))
    wanted = jnp.pad(wanted, ((0, 0), (0, 8 - capacity), (0, 0)), constant_values=-1)
    table = database.reshape(database.shape[0] * length, enc_width)
    arrived, key_weight, value_weight = fetch(
        wanted, table, key_weight, value_weight, length, lax.axis_size("dp")
    )
    arrived = arrived.reshape(owners * capacity, length, enc_width)
    fetched = jnp.take(arrived, shard_flat * capacity + slot_rank, axis=0).reshape(
        spans, nbr_count, length, enc_width
    )
    prior_rows = from_behind(fetched[-1:], ("dp", "seq"), 1)
    keys_own, values_own = project(fetched, enc_gain, key_weight, value_weight)
    keys_prior, values_prior = project(prior_rows, enc_gain, key_weight, value_weight)
    keys_all = jnp.concatenate([keys_prior, keys_own], axis=0)
    values_all = jnp.concatenate([values_prior, values_own], axis=0)
    token_count = queries.shape[0]
    columns = queries.shape[1]
    padded = jnp.concatenate(
        [
            jnp.zeros((1, columns), queries.dtype),
            queries,
            jnp.zeros((SPAN - 1, columns), queries.dtype),
        ],
        axis=0,
    )
    grouped = padded.reshape(spans + 1, SPAN, columns)
    return attend(grouped, keys_all, values_all)[1 : 1 + token_count]


def solution(mesh):
    return jax.shard_map(
        body,
        mesh=mesh,
        in_specs=(
            P(("dp", "seq"), None),
            P("seq", None, None),
            P(),
            P(None, "dp"),
            P(None, "dp"),
            P(("dp", "seq"), None),
            P(("dp", "seq"), None),
        ),
        out_specs=P(("dp", "seq"), None),
        check_vma=False,
    )
```

```python
import functools
import math

import jax
import jax.numpy as jnp
from jax import lax
from jax.experimental import pallas as pl
from jax.experimental.pallas import tpu as pltpu
from jax.sharding import PartitionSpec as P

MESH = pl.DeviceIdType.MESH

HEADS = 16
DH = 128
SPAN = 64


eps_norm = 1e-06


def from_behind(block, axis, distance):
    devices = range(lax.axis_size(axis))
    route = [(i - distance, i) for i in devices if i - distance in devices]
    return lax.ppermute(block, axis, route)


def gathered_rows(ids_list, table_ref, length):
    pieces = []
    for ids in ids_list:
        for slot in range(2):
            pieces.append(jnp.broadcast_to(ids[slot : slot + 1, :], (length, 128)))
    sel = jnp.concatenate(pieces, axis=0)
    shape = sel.shape
    sub = lax.broadcasted_iota(jnp.int32, shape, 0)
    lane = lax.broadcasted_iota(jnp.int32, shape, 1)
    total = jnp.zeros((shape[0], table_ref.shape[1]), jnp.float32)
    for h in range(table_ref.shape[0] // 128):
        col = lane + h * 128
        hit = jnp.logical_and(col // length == sel, col % length == sub % length)
        total += jnp.dot(
            hit.astype(table_ref.dtype),
            table_ref[h * 128 : (h + 1) * 128, :],
            preferred_element_type=jnp.float32,
        )
    return total.astype(table_ref.dtype)


def torus_step(k, across, depth, sign):
    i = lax.rem(depth - k // across, depth)
    j = lax.rem(k, across)
    dz = sign * ((i + 1) // 2) * (2 * lax.rem(i, 2) - 1)
    dy = sign * ((j + 1) // 2) * (2 * lax.rem(j, 2) - 1)
    return dy, dz


def fetch_kernel(
    length, group, wanted_ref, table_ref, wk_ref, wv_ref, out_ref, wk_out, wv_out,
    asked, outgoing, req_send, req_recv, rep_send, rep_recv, wk_send, wk_recv, wv_send, wv_recv, own_sem,
):
    n = wanted_ref.shape[0]
    nd = wk_out.shape[1] // wk_ref.shape[1]
    me = lax.axis_index("seq")
    dp = lax.axis_index("dp")
    across = math.gcd(4, n)
    depth = n // across

    def peer_of(k, sign):
        dy, dz = torus_step(k, across, depth, sign)
        y = lax.rem(me, across)
        z = me // across
        return lax.rem(z + dz + depth, depth) * across + lax.rem(y + dy + across, across)

    def request(peer, slot):
        return pltpu.make_async_remote_copy(
            wanted_ref.at[peer], asked.at[slot], req_send.at[peer], req_recv.at[slot],
            device_id=(dp, peer), device_id_type=MESH,
        )

    def reply(step, peer, slot):
        return pltpu.make_async_remote_copy(
            outgoing.at[step], out_ref.at[slot], rep_send.at[step], rep_recv.at[slot],
            device_id=(dp, peer), device_id_type=MESH,
        )

    cols = wk_ref.shape[1]

    def weight(src, dst, send, recv, peer, slot):
        return pltpu.make_async_remote_copy(
            src, dst.at[:, pl.ds(slot * cols, cols)], send.at[peer], recv.at[slot],
            device_id=(peer, me), device_id_type=MESH,
        )

    def weights(peer, slot):
        return (
            weight(wk_ref, wk_out, wk_send, wk_recv, peer, slot),
            weight(wv_ref, wv_out, wv_send, wv_recv, peer, slot),
        )

    own = (
        pltpu.make_async_copy(wk_ref, wk_out.at[:, pl.ds(dp * cols, cols)], own_sem.at[0]),
        pltpu.make_async_copy(wv_ref, wv_out.at[:, pl.ds(dp * cols, cols)], own_sem.at[1]),
    )

    barrier = pltpu.get_barrier_semaphore()

    def greet(k, carry):
        pl.semaphore_signal(barrier, inc=1, device_id=(dp, lax.rem(me + k, n)), device_id_type=MESH)
        return carry

    def greet_dp(k, carry):
        pl.semaphore_signal(barrier, inc=1, device_id=(lax.rem(dp + k, nd), me), device_id_type=MESH)
        return carry

    lax.fori_loop(1, n, greet, 0)
    lax.fori_loop(1, nd, greet_dp, 0)
    pl.semaphore_wait(barrier, n - 1 + nd - 1)

    def share(k, carry):
        for copy in weights(lax.rem(dp + k, nd), dp):
            copy.start()
        return carry

    lax.fori_loop(1, nd, share, 0)
    for copy in own:
        copy.start()

    def ask(k, carry):
        request(peer_of(k, 1), me).start()
        return carry

    lax.fori_loop(1, n, ask, 0)

    asked[me] = wanted_ref[me]

    def serve(c, carry):
        ids_list = []
        for j in range(group):
            k = c * group + j
            source = peer_of(k, -1)

            @pl.when(k > 0)
            def _():
                request(source, source).wait_recv()

            ids_list.append(asked[source])
        rows = gathered_rows(ids_list, table_ref, length)
        outgoing[pl.ds(c * group, group)] = rows.reshape(group, 2 * length, rows.shape[-1])
        for j in range(group):
            k = c * group + j
            source = peer_of(k, -1)

            @pl.when(k == 0)
            def _():
                pltpu.make_async_copy(outgoing.at[k], out_ref.at[me], own_sem.at[2]).start()

            @pl.when(k > 0)
            def _():
                reply(k, source, me).start()

        return carry

    lax.fori_loop(0, n // group, serve, 0)

    def finish(k, carry):
        peer = peer_of(k, 1)
        request(peer, me).wait_send()
        reply(k, peer_of(k, -1), me).wait_send()
        reply(k, peer, peer).wait_recv()
        return carry

    lax.fori_loop(1, n, finish, 0)

    def gathered(k, carry):
        peer = lax.rem(dp + k, nd)
        for copy in weights(peer, dp):
            copy.wait_send()
        for copy in weights(peer, peer):
            copy.wait_recv()
        return carry

    lax.fori_loop(1, nd, gathered, 0)
    for copy in own:
        copy.wait()
    pltpu.make_async_copy(outgoing.at[0], out_ref.at[me], own_sem.at[2]).wait()


def fetch(wanted, table, key_weight, value_weight, length, nd):
    n = wanted.shape[0]
    width = table.shape[1]
    vmem = pl.BlockSpec(memory_space=pltpu.VMEM)
    anywhere = pl.BlockSpec(memory_space=pl.ANY)
    return pl.pallas_call(
        functools.partial(fetch_kernel, length, math.gcd(8, n)),
        out_shape=(
            jax.ShapeDtypeStruct((n, 2 * length, width), table.dtype),
            jax.ShapeDtypeStruct((key_weight.shape[0], nd * key_weight.shape[1]), key_weight.dtype),
            jax.ShapeDtypeStruct((value_weight.shape[0], nd * value_weight.shape[1]), value_weight.dtype),
        ),
        in_specs=[vmem, vmem, anywhere, anywhere],
        out_specs=(anywhere, anywhere, anywhere),
        scratch_shapes=[
            pltpu.VMEM(wanted.shape, jnp.int32),
            pltpu.VMEM((n, 2 * length, width), table.dtype),
            pltpu.SemaphoreType.DMA((n,)),
            pltpu.SemaphoreType.DMA((n,)),
            pltpu.SemaphoreType.DMA((n,)),
            pltpu.SemaphoreType.DMA((n,)),
            pltpu.SemaphoreType.DMA((nd,)),
            pltpu.SemaphoreType.DMA((nd,)),
            pltpu.SemaphoreType.DMA((nd,)),
            pltpu.SemaphoreType.DMA((nd,)),
            pltpu.SemaphoreType.DMA((3,)),
        ],
        compiler_params=pltpu.CompilerParams(collective_id=0, has_side_effects=True),
    )(wanted, table, key_weight, value_weight)


def normalize(nbr_rows, enc_gain):
    widened = nbr_rows.astype(jnp.float32)
    mean_square = jnp.mean(widened * widened, axis=-1, keepdims=True)
    return (widened * lax.rsqrt(mean_square + eps_norm) * enc_gain).astype(jnp.bfloat16)


def project(nbr_rows, enc_gain, key_weight, value_weight):
    group_count = nbr_rows.shape[0]
    normed = normalize(nbr_rows, enc_gain)
    flat_rows = normed.reshape(-1, normed.shape[-1])
    key_part = jnp.dot(flat_rows, key_weight, preferred_element_type=jnp.float32)
    value_part = jnp.dot(flat_rows, value_weight, preferred_element_type=jnp.float32)
    keys_out = key_part.astype(jnp.bfloat16)
    values_out = value_part.astype(jnp.bfloat16)
    return (
        keys_out.reshape(group_count, -1, keys_out.shape[-1]),
        values_out.reshape(group_count, -1, values_out.shape[-1]),
    )


def attend(grouped, keys_in, values_in):
    group_count = grouped.shape[0]
    query_heads = grouped.reshape(group_count, SPAN, HEADS, DH)
    key_heads = keys_in.reshape(group_count, -1, HEADS, DH)
    value_heads = values_in.reshape(group_count, -1, HEADS, DH)
    scores = jnp.einsum(
        "gqhd,gkhd->ghqk", query_heads, key_heads, preferred_element_type=jnp.float32
    ) * (1.0 / math.sqrt(DH))
    row_max = jnp.max(scores, axis=-1, keepdims=True)
    expo = jnp.exp(scores - row_max)
    probs_low = (expo / jnp.sum(expo, axis=-1, keepdims=True)).astype(jnp.bfloat16)
    mixed = jnp.einsum(
        "ghqk,gkhd->gqhd", probs_low, value_heads, preferred_element_type=jnp.float32
    )
    return mixed.reshape(group_count * SPAN, HEADS * DH).astype(jnp.bfloat16)


def body(queries, database, enc_gain, key_weight, value_weight, ret_shard, ret_row):
    spans = ret_shard.shape[0]
    nbr_count = ret_shard.shape[1]
    owners = lax.axis_size("seq")
    capacity = max(2, min(spans, 2 * spans * nbr_count // owners))
    requests = spans * nbr_count
    length = database.shape[1]
    enc_width = database.shape[2]
    shard_flat = ret_shard.reshape(requests)
    row_flat = ret_row.reshape(requests)
    order = jnp.arange(requests, dtype=jnp.int32)
    same_owner = shard_flat[:, None] == shard_flat[None, :]
    earlier = order[None, :] < order[:, None]
    slot_rank = jnp.sum(jnp.logical_and(same_owner, earlier), axis=1)
    owner_ids = jnp.arange(owners, dtype=jnp.int32)
    slot_ids = jnp.arange(capacity, dtype=jnp.int32)
    matches = jnp.logical_and(
        shard_flat[None, None, :] == owner_ids[:, None, None],
        slot_rank[None, None, :] == slot_ids[None, :, None],
    )
    wanted = jnp.sum(jnp.where(matches, row_flat[None, None, :] + 1, 0), axis=2) - 1
    wanted = jnp.broadcast_to(wanted[:, :, None], (owners, capacity, 128))
    wanted = jnp.pad(wanted, ((0, 0), (0, 8 - capacity), (0, 0)), constant_values=-1)
    table = database.reshape(database.shape[0] * length, enc_width)
    arrived, key_weight, value_weight = fetch(
        wanted, table, key_weight, value_weight, length, lax.axis_size("dp")
    )
    arrived = arrived.reshape(owners * capacity, length, enc_width)
    fetched = jnp.take(arrived, shard_flat * capacity + slot_rank, axis=0).reshape(
        spans, nbr_count, length, enc_width
    )
    last_slots = (shard_flat * capacity + slot_rank)[requests - nbr_count :]
    last_rows = jnp.take(arrived, last_slots, axis=0)[None]
    prior_rows = from_behind(last_rows, ("dp", "seq"), 1)
    keys_own, values_own = project(fetched, enc_gain, key_weight, value_weight)
    keys_prior, values_prior = project(prior_rows, enc_gain, key_weight, value_weight)
    keys_all = jnp.concatenate([keys_prior, keys_own], axis=0)
    values_all = jnp.concatenate([values_prior, values_own], axis=0)
    token_count = queries.shape[0]
    columns = queries.shape[1]
    padded = jnp.concatenate(
        [
            jnp.zeros((1, columns), queries.dtype),
            queries,
            jnp.zeros((SPAN - 1, columns), queries.dtype),
        ],
        axis=0,
    )
    grouped = padded.reshape(spans + 1, SPAN, columns)
    return attend(grouped, keys_all, values_all)[1 : 1 + token_count]


def solution(mesh):
    return jax.shard_map(
        body,
        mesh=mesh,
        in_specs=(
            P(("dp", "seq"), None),
            P("seq", None, None),
            P(),
            P(None, "dp"),
            P(None, "dp"),
            P(("dp", "seq"), None),
            P(("dp", "seq"), None),
        ),
        out_specs=P(("dp", "seq"), None),
        check_vma=False,
    )
```

```python
import functools
import math

import jax
import jax.numpy as jnp
from jax import lax
from jax.experimental import pallas as pl
from jax.experimental.pallas import tpu as pltpu
from jax.sharding import PartitionSpec as P

MESH = pl.DeviceIdType.MESH

HEADS = 16
DH = 128
SPAN = 64


eps_norm = 1e-06


def from_behind(block, axis, distance):
    devices = range(lax.axis_size(axis))
    route = [(i - distance, i) for i in devices if i - distance in devices]
    return lax.ppermute(block, axis, route)


def gathered_rows(ids_list, table_ref, length):
    pieces = []
    for ids in ids_list:
        for slot in range(2):
            pieces.append(jnp.broadcast_to(ids[slot : slot + 1, :], (length, 128)))
    sel = jnp.concatenate(pieces, axis=0)
    shape = sel.shape
    sub = lax.broadcasted_iota(jnp.int32, shape, 0)
    lane = lax.broadcasted_iota(jnp.int32, shape, 1)
    total = jnp.zeros((shape[0], table_ref.shape[1]), jnp.float32)
    for h in range(table_ref.shape[0] // 128):
        col = lane + h * 128
        hit = jnp.logical_and(col // length == sel, col % length == sub % length)
        total += jnp.dot(
            hit.astype(table_ref.dtype),
            table_ref[h * 128 : (h + 1) * 128, :],
            preferred_element_type=jnp.float32,
        )
    return total.astype(table_ref.dtype)


def torus_step(k, across, depth, sign):
    i = lax.rem(depth - k // across, depth)
    j = lax.rem(k, across)
    dz = sign * ((i + 1) // 2) * (2 * lax.rem(i, 2) - 1)
    dy = sign * ((j + 1) // 2) * (2 * lax.rem(j, 2) - 1)
    return dy, dz


def fetch_kernel(
    length, group, wanted_ref, table_ref, wk_ref, wv_ref, out_ref, wk_out, wv_out,
    asked, outgoing, req_send, req_recv, rep_send, rep_recv, wk_send, wk_recv, wv_send, wv_recv, wk_fwd, wv_fwd,
    own_sem,
):
    n = wanted_ref.shape[0]
    nd = wk_out.shape[1] // wk_ref.shape[1]
    me = lax.axis_index("seq")
    dp = lax.axis_index("dp")
    across = math.gcd(4, n)
    depth = n // across

    def peer_of(k, sign):
        dy, dz = torus_step(k, across, depth, sign)
        y = lax.rem(me, across)
        z = me // across
        return lax.rem(z + dz + depth, depth) * across + lax.rem(y + dy + across, across)

    def request(peer, slot):
        return pltpu.make_async_remote_copy(
            wanted_ref.at[peer], asked.at[slot], req_send.at[peer], req_recv.at[slot],
            device_id=(dp, peer), device_id_type=MESH,
        )

    def reply(step, peer, slot):
        return pltpu.make_async_remote_copy(
            outgoing.at[step], out_ref.at[slot], rep_send.at[step], rep_recv.at[slot],
            device_id=(dp, peer), device_id_type=MESH,
        )

    cols = wk_ref.shape[1]
    partner = dp + 1 - 2 * lax.rem(dp, 2)
    pairs = nd // 2

    def weights(src_k, src_v, peer, slot, sent_k, sent_v, sent_slot):
        return [
            pltpu.make_async_remote_copy(
                src, dst.at[:, pl.ds(slot * cols, cols)], sent.at[sent_slot], recv.at[slot],
                device_id=(peer, me), device_id_type=MESH,
            )
            for src, dst, sent, recv in ((src_k, wk_out, sent_k, wk_recv), (src_v, wv_out, sent_v, wv_recv))
        ]

    def own_shard(peer):
        return weights(wk_ref, wv_ref, peer, dp, wk_send, wv_send, peer)

    def relayed(slot, peer):
        return weights(
            wk_out.at[:, pl.ds(slot * cols, cols)], wv_out.at[:, pl.ds(slot * cols, cols)],
            peer, slot, wk_fwd, wv_fwd, slot,
        )

    own = (
        pltpu.make_async_copy(wk_ref, wk_out.at[:, pl.ds(dp * cols, cols)], own_sem.at[0]),
        pltpu.make_async_copy(wv_ref, wv_out.at[:, pl.ds(dp * cols, cols)], own_sem.at[1]),
    )

    barrier = pltpu.get_barrier_semaphore()

    def greet(k, carry):
        pl.semaphore_signal(barrier, inc=1, device_id=(dp, lax.rem(me + k, n)), device_id_type=MESH)
        return carry

    def greet_dp(k, carry):
        pl.semaphore_signal(barrier, inc=1, device_id=(lax.rem(dp + k, nd), me), device_id_type=MESH)
        return carry

    lax.fori_loop(1, n, greet, 0)
    lax.fori_loop(1, nd, greet_dp, 0)
    pl.semaphore_wait(barrier, n - 1 + nd - 1)

    def share(m, carry):
        for copy in own_shard(lax.rem(dp + 2 * m, nd)):
            copy.start()
        return carry

    for copy in own_shard(partner):
        copy.start()
    lax.fori_loop(1, pairs, share, 0)
    for copy in own:
        copy.start()

    def ask(k, carry):
        request(peer_of(k, 1), me).start()
        return carry

    lax.fori_loop(1, n, ask, 0)

    asked[me] = wanted_ref[me]

    def serve(c, carry):
        ids_list = []
        for j in range(group):
            k = c * group + j
            source = peer_of(k, -1)

            @pl.when(k > 0)
            def _():
                request(source, source).wait_recv()

            ids_list.append(asked[source])
        rows = gathered_rows(ids_list, table_ref, length)
        outgoing[pl.ds(c * group, group)] = rows.reshape(group, 2 * length, rows.shape[-1])
        for j in range(group):
            k = c * group + j
            source = peer_of(k, -1)

            @pl.when(k == 0)
            def _():
                pltpu.make_async_copy(outgoing.at[k], out_ref.at[me], own_sem.at[2]).start()

            @pl.when(k > 0)
            def _():
                reply(k, source, me).start()

        return carry

    lax.fori_loop(0, n // group, serve, 0)

    def relay(m, carry):
        slot = lax.rem(dp + 2 * m, nd)
        for copy in relayed(slot, partner):
            copy.wait_recv()
        for copy in relayed(slot, partner):
            copy.start()
        return carry

    lax.fori_loop(1, pairs, relay, 0)

    def finish(k, carry):
        peer = peer_of(k, 1)
        request(peer, me).wait_send()
        reply(k, peer_of(k, -1), me).wait_send()
        reply(k, peer, peer).wait_recv()
        return carry

    lax.fori_loop(1, n, finish, 0)

    def gathered(m, carry):
        peer = lax.rem(dp + 2 * m, nd)
        for copy in own_shard(peer):
            copy.wait_send()
        for copy in relayed(peer, partner):
            copy.wait_send()
        for copy in relayed(lax.rem(partner + 2 * m, nd), partner):
            copy.wait_recv()
        return carry

    lax.fori_loop(1, pairs, gathered, 0)
    for copy in own_shard(partner):
        copy.wait_send()
    for copy in relayed(partner, partner):
        copy.wait_recv()
    for copy in own:
        copy.wait()
    pltpu.make_async_copy(outgoing.at[0], out_ref.at[me], own_sem.at[2]).wait()


def fetch(wanted, table, key_weight, value_weight, length, nd):
    n = wanted.shape[0]
    width = table.shape[1]
    vmem = pl.BlockSpec(memory_space=pltpu.VMEM)
    anywhere = pl.BlockSpec(memory_space=pl.ANY)
    return pl.pallas_call(
        functools.partial(fetch_kernel, length, math.gcd(8, n)),
        out_shape=(
            jax.ShapeDtypeStruct((n, 2 * length, width), table.dtype),
            jax.ShapeDtypeStruct((key_weight.shape[0], nd * key_weight.shape[1]), key_weight.dtype),
            jax.ShapeDtypeStruct((value_weight.shape[0], nd * value_weight.shape[1]), value_weight.dtype),
        ),
        in_specs=[vmem, vmem, anywhere, anywhere],
        out_specs=(anywhere, anywhere, anywhere),
        scratch_shapes=[
            pltpu.VMEM(wanted.shape, jnp.int32),
            pltpu.VMEM((n, 2 * length, width), table.dtype),
            pltpu.SemaphoreType.DMA((n,)),
            pltpu.SemaphoreType.DMA((n,)),
            pltpu.SemaphoreType.DMA((n,)),
            pltpu.SemaphoreType.DMA((n,)),
            pltpu.SemaphoreType.DMA((nd,)),
            pltpu.SemaphoreType.DMA((nd,)),
            pltpu.SemaphoreType.DMA((nd,)),
            pltpu.SemaphoreType.DMA((nd,)),
            pltpu.SemaphoreType.DMA((nd,)),
            pltpu.SemaphoreType.DMA((nd,)),
            pltpu.SemaphoreType.DMA((3,)),
        ],
        compiler_params=pltpu.CompilerParams(collective_id=0, has_side_effects=True),
    )(wanted, table, key_weight, value_weight)


def normalize(nbr_rows, enc_gain):
    widened = nbr_rows.astype(jnp.float32)
    mean_square = jnp.mean(widened * widened, axis=-1, keepdims=True)
    return (widened * lax.rsqrt(mean_square + eps_norm) * enc_gain).astype(jnp.bfloat16)


def project(nbr_rows, enc_gain, key_weight, value_weight):
    group_count = nbr_rows.shape[0]
    normed = normalize(nbr_rows, enc_gain)
    flat_rows = normed.reshape(-1, normed.shape[-1])
    key_part = jnp.dot(flat_rows, key_weight, preferred_element_type=jnp.float32)
    value_part = jnp.dot(flat_rows, value_weight, preferred_element_type=jnp.float32)
    keys_out = key_part.astype(jnp.bfloat16)
    values_out = value_part.astype(jnp.bfloat16)
    return (
        keys_out.reshape(group_count, -1, keys_out.shape[-1]),
        values_out.reshape(group_count, -1, values_out.shape[-1]),
    )


def attend(grouped, keys_in, values_in):
    group_count = grouped.shape[0]
    query_heads = grouped.reshape(group_count, SPAN, HEADS, DH)
    key_heads = keys_in.reshape(group_count, -1, HEADS, DH)
    value_heads = values_in.reshape(group_count, -1, HEADS, DH)
    scores = jnp.einsum(
        "gqhd,gkhd->ghqk", query_heads, key_heads, preferred_element_type=jnp.float32
    ) * (1.0 / math.sqrt(DH))
    row_max = jnp.max(scores, axis=-1, keepdims=True)
    expo = jnp.exp(scores - row_max)
    probs_low = (expo / jnp.sum(expo, axis=-1, keepdims=True)).astype(jnp.bfloat16)
    mixed = jnp.einsum(
        "ghqk,gkhd->gqhd", probs_low, value_heads, preferred_element_type=jnp.float32
    )
    return mixed.reshape(group_count * SPAN, HEADS * DH).astype(jnp.bfloat16)


def body(queries, database, enc_gain, key_weight, value_weight, ret_shard, ret_row):
    spans = ret_shard.shape[0]
    nbr_count = ret_shard.shape[1]
    owners = lax.axis_size("seq")
    capacity = max(2, min(spans, 2 * spans * nbr_count // owners))
    requests = spans * nbr_count
    length = database.shape[1]
    enc_width = database.shape[2]
    shard_flat = ret_shard.reshape(requests)
    row_flat = ret_row.reshape(requests)
    order = jnp.arange(requests, dtype=jnp.int32)
    same_owner = shard_flat[:, None] == shard_flat[None, :]
    earlier = order[None, :] < order[:, None]
    slot_rank = jnp.sum(jnp.logical_and(same_owner, earlier), axis=1)
    owner_ids = jnp.arange(owners, dtype=jnp.int32)
    slot_ids = jnp.arange(capacity, dtype=jnp.int32)
    matches = jnp.logical_and(
        shard_flat[None, None, :] == owner_ids[:, None, None],
        slot_rank[None, None, :] == slot_ids[None, :, None],
    )
    wanted = jnp.sum(jnp.where(matches, row_flat[None, None, :] + 1, 0), axis=2) - 1
    wanted = jnp.broadcast_to(wanted[:, :, None], (owners, capacity, 128))
    wanted = jnp.pad(wanted, ((0, 0), (0, 8 - capacity), (0, 0)), constant_values=-1)
    table = database.reshape(database.shape[0] * length, enc_width)
    arrived, key_weight, value_weight = fetch(
        wanted, table, key_weight, value_weight, length, lax.axis_size("dp")
    )
    arrived = arrived.reshape(owners * capacity, length, enc_width)
    fetched = jnp.take(arrived, shard_flat * capacity + slot_rank, axis=0).reshape(
        spans, nbr_count, length, enc_width
    )
    prior_rows = from_behind(fetched[-1:], ("dp", "seq"), 1)
    keys_own, values_own = project(fetched, enc_gain, key_weight, value_weight)
    keys_prior, values_prior = project(prior_rows, enc_gain, key_weight, value_weight)
    keys_all = jnp.concatenate([keys_prior, keys_own], axis=0)
    values_all = jnp.concatenate([values_prior, values_own], axis=0)
    token_count = queries.shape[0]
    columns = queries.shape[1]
    padded = jnp.concatenate(
        [
            jnp.zeros((1, columns), queries.dtype),
            queries,
            jnp.zeros((SPAN - 1, columns), queries.dtype),
        ],
        axis=0,
    )
    grouped = padded.reshape(spans + 1, SPAN, columns)
    return attend(grouped, keys_all, values_all)[1 : 1 + token_count]


def solution(mesh):
    return jax.shard_map(
        body,
        mesh=mesh,
        in_specs=(
            P(("dp", "seq"), None),
            P("seq", None, None),
            P(),
            P(None, "dp"),
            P(None, "dp"),
            P(("dp", "seq"), None),
            P(("dp", "seq"), None),
        ),
        out_specs=P(("dp", "seq"), None),
        check_vma=False,
    )
```
